256 devices in a mesh: col: 8 (over z), row: 32 (over y, x, core).
Axes of the slice: x: 4, y: 4, z: 8, core: 2. Of those that a mesh axis runs over, the one named last changes fastest.
Arguments:
- queries: bfloat16 [262144, 256], P(('col', 'row')), may hold values from -6 to 6
- keys: bfloat16 [262144, 256], P(('col', 'row')), may hold values from -6 to 6
- values: bfloat16 [262144, 256], P(('col', 'row')), may hold values from -6 to 6
- out_grad: bfloat16 [262144, 256], P(('col', 'row')), may hold values from -6 to 6
- weight_table: float32 [64, 2, 21], replicated, may hold values from 0.25 to 2
- profile: int32 [262144], P(('col', 'row')), may hold values from 0 to 63
Outputs:
- output: float32 [262144, 256], P(('col', 'row'))
- query_grad: float32 [262144, 256], P(('col', 'row'))
- key_grad: float32 [262144, 256], P(('col', 'row'))
- value_grad: float32 [262144, 256], P(('col', 'row'))
The draws below stay inside these ranges and needn't reach their ends.
All inputs are finite; a program needn't handle non-finite values.
Results may differ from the reference program's by a relative error of at most 0.0034.
Values sent between devices are 32-bit elements; how exact they have to be, the bound alone decides.
No kernel may reach another device: no remote copies, remote signals or barrier semaphores. Data moves between devices by JAX's collectives and lax.ppermute only.
A program may use at most 128 MiB of HBM per device.

```python
import math
import jax
import jax.numpy as jnp
from jax import lax

H = 2
DH = 128
LEVELS = 21
PROFILES = 64
SEQ = 262144
N_COL = 8
N_ROW = 32


def with_ends(array, own_key, smallest, high):
    shape = array.shape
    spot = [jax.random.randint(jax.random.fold_in(own_key, axis), (), 0, shape[axis]) for axis in range(len(shape))]
    array = array.at[tuple(spot)].set(smallest)
    longest = shape.index(max(shape))
    spot[longest] = (spot[longest] + 1) % shape[longest]
    return array.at[tuple(spot)].set(high)


def shard_levels(key, extent, split, low, largest):
    def one(position, shards_of):
        steps = jax.random.uniform(jax.random.fold_in(jax.random.fold_in(key, 6), position), (shards_of,), jnp.float32, low / len(split), largest / len(split))
        return jnp.repeat(jnp.exp(steps), extent[position] // shards_of).reshape((-1,) + (1,) * (len(extent) - position - 1))

    gain = one(*split[0])
    for cut in split[1:]:
        gain = gain * one(*cut)
    return gain


def scatter_about(rng, dims, scale, most, shards=(), kind=jnp.bfloat16):
    array = scale * jax.random.normal(rng, dims, jnp.float32)
    if shards:
        array = array * shard_levels(rng, dims, shards, -0.22, 0.18)
    return jnp.clip(array, -most, most).astype(kind)


def setup_inputs(seed: int = 0) -> dict:
    key_of = jax.random.split(jax.random.key(seed), 7)
    return {
        "queries": scatter_about(key_of[0], (SEQ, H * DH), 1.0, 6.0, ((0, 256),)),
        "keys": scatter_about(key_of[1], (SEQ, H * DH), 1.0, 6.0, ((0, 256),)),
        "values": scatter_about(key_of[2], (SEQ, H * DH), 1.0, 6.0, ((0, 256),)),
        "out_grad": scatter_about(key_of[3], (SEQ, H * DH), 1.0, 6.0, ((0, 256),)),
        "weight_table": jnp.clip(jnp.exp(jax.random.uniform(key_of[4], (PROFILES, H, LEVELS), jnp.float32, math.log(0.25), math.log(2.0))), 0.25, 2.0),
        "profile": with_ends(jax.random.randint(key_of[5], (SEQ,), 0, PROFILES), jax.random.fold_in(key_of[5], 1), 0, PROFILES - 1).astype(jnp.int32),
    }


HIGHEST_PRECISION = lax.Precision.HIGHEST

def digit_count(numbers, count):
    total = jnp.zeros_like(numbers)
    for digit_place in range(count):
        total = total + (numbers >= 1 << digit_place).astype(jnp.int32)
    return total

def level_weights(weight_table, profile, head_width):
    table_rows = weight_table.shape[0]
    onehot = (profile[:, None] == jnp.arange(table_rows, dtype=jnp.int32)[None, :]).astype(jnp.float32)
    flat_table = weight_table.reshape(table_rows, -1)
    picked = jnp.dot(onehot, flat_table, precision=HIGHEST_PRECISION, preferred_element_type=jnp.float32)
    picked = picked.reshape(profile.shape[0], weight_table.shape[1], weight_table.shape[2])
    depth = jnp.arange(weight_table.shape[2], dtype=jnp.float32)
    scaling = jnp.exp2(-0.5 * depth) / math.sqrt(head_width)
    return picked * scaling

def sibling_sums(states, bit_place, receiver):
    count = states.shape[0]
    remain = states.shape[1:]
    shape = (count >> bit_place + 1, 2, 1 << bit_place) + remain
    grouped = lax.optimization_barrier(jnp.sum(states.reshape(shape), axis=2))
    source = grouped[:, 1 - receiver]
    empty = jnp.zeros_like(source)
    halves = [source, empty] if receiver == 0 else [empty, source]
    paired = jnp.stack(halves, axis=1)
    spread = jnp.broadcast_to(paired[:, :, None], shape)
    return spread.reshape(states.shape)

def tile_local(query_heads, key_heads, value_heads, grad_heads, weights, tile_bits):
    count = query_heads.shape[0]
    places = jnp.arange(count, dtype=jnp.int32)
    levels = digit_count(jnp.bitwise_xor(places[:, None], places[None, :]), tile_bits)
    causal = places[None, :] <= places[:, None]
    level_mask = jnp.zeros((query_heads.shape[1], count, count), jnp.float32)
    for level in range(tile_bits + 1):
        level_mask = level_mask + jnp.where(levels[None] == level, jnp.transpose(weights[:, :, level])[:, :, None], 0.0)
    level_mask = jnp.where(causal[None], level_mask, 0.0)
    query_f = query_heads.astype(jnp.float32)
    key_f = key_heads.astype(jnp.float32)
    value_f = value_heads.astype(jnp.float32)
    grad_f = grad_heads.astype(jnp.float32)
    scores = jnp.einsum('thd,shd->hts', query_f, key_f, precision=HIGHEST_PRECISION)
    local_probs = (scores * level_mask).astype(jnp.bfloat16)
    probs_f = local_probs.astype(jnp.float32)
    local_out = jnp.einsum('hts,she->the', probs_f, value_f, precision=HIGHEST_PRECISION)
    grad_scores = jnp.einsum('the,she->hts', grad_f, value_f, precision=HIGHEST_PRECISION)
    local_grad = (grad_scores * level_mask).astype(jnp.bfloat16).astype(jnp.float32)
    local_dq = jnp.einsum('hts,shd->thd', local_grad, key_f, precision=HIGHEST_PRECISION)
    local_dk = jnp.einsum('hts,thd->shd', local_grad, query_f, precision=HIGHEST_PRECISION)
    local_dv = jnp.einsum('hts,the->she', probs_f, grad_f, precision=HIGHEST_PRECISION)
    return (local_out, local_dq, local_dk, local_dv)

def tile_far(query_heads, key_heads, value_heads, grad_heads, far_weights, bucket_half, pulled_half):
    query_f = query_heads.astype(jnp.float32)
    key_f = key_heads.astype(jnp.float32)
    value_f = value_heads.astype(jnp.float32)
    grad_f = grad_heads.astype(jnp.float32)
    bucket_f = bucket_half.astype(jnp.float32)
    pulled_f = pulled_half.astype(jnp.float32)
    reach = jnp.einsum('thd,lhde->thle', query_f, bucket_f, precision=HIGHEST_PRECISION)
    far_out = lax.optimization_barrier(jnp.sum(reach * far_weights[..., None], axis=2))
    back = jnp.einsum('the,lhde->thld', grad_f, bucket_f, precision=HIGHEST_PRECISION)
    far_dq = lax.optimization_barrier(jnp.sum(back * far_weights[..., None], axis=2))
    far_dk = jnp.einsum('the,hde->thd', value_f, pulled_f, precision=HIGHEST_PRECISION)
    far_dv = jnp.einsum('thd,hde->the', key_f, pulled_f, precision=HIGHEST_PRECISION)
    return (far_out, far_dq, far_dk, far_dv)

def tile_grad_state(query_heads, grad_heads, far_weights):
    weighted = (query_heads.astype(jnp.float32)[:, :, None, :] * far_weights[..., None]).astype(jnp.bfloat16)
    return jnp.einsum('thld,the->lhde', weighted.astype(jnp.float32), grad_heads.astype(jnp.float32), precision=HIGHEST_PRECISION)

def reference(queries, keys, values, out_grad, weight_table, profile):
    tile_count = N_COL * N_ROW
    token_count = queries.shape[0] // tile_count
    head_count = weight_table.shape[1]
    head_width = queries.shape[1] // head_count
    tile_bits = token_count.bit_length() - 1
    far_levels = tile_count.bit_length() - 1
    weights = level_weights(weight_table, profile, head_width).reshape(tile_count, token_count, head_count, -1)
    far_weights = weights[:, :, :, tile_bits + 1:tile_bits + 1 + far_levels]
    tile_shape = (tile_count, token_count, head_count, head_width)
    query_tiles = queries.reshape(tile_shape)
    key_tiles = keys.reshape(tile_shape)
    value_tiles = values.reshape(tile_shape)
    grad_tiles = out_grad.reshape(tile_shape)
    tile_state = jnp.einsum('bthd,bthe->bhde', key_tiles.astype(jnp.float32), value_tiles.astype(jnp.float32), precision=HIGHEST_PRECISION)

    def grad_of_tile(items):
        return tile_grad_state(items[0], items[1], items[2])
    grad_state = lax.map(grad_of_tile, (query_tiles, grad_tiles, far_weights))
    bucket = jnp.stack([sibling_sums(tile_state, level, 1) for level in range(far_levels)], axis=1)
    bucket_half = bucket.astype(jnp.bfloat16)
    pulled = jnp.zeros_like(tile_state)
    for level in range(far_levels):
        pulled = pulled + sibling_sums(grad_state[:, level], level, 0)
    pulled_half = pulled.astype(jnp.bfloat16)

    def per_tile(items):
        query_heads, key_heads, value_heads, grad_heads, tile_weights, bucket_tile, pulled_tile = items
        local_out, local_dq, local_dk, local_dv = tile_local(query_heads, key_heads, value_heads, grad_heads, tile_weights, tile_bits)
        far_out, far_dq, far_dk, far_dv = tile_far(query_heads, key_heads, value_heads, grad_heads, tile_weights[:, :, tile_bits + 1:tile_bits + 1 + far_levels], bucket_tile, pulled_tile)
        return (local_out + far_out, local_dq + far_dq, local_dk + far_dk, local_dv + far_dv)
    results = lax.map(per_tile, (query_tiles, key_tiles, value_tiles, grad_tiles, weights, bucket_half, pulled_half))
    return (results[0].reshape(queries.shape), results[1].reshape(queries.shape), results[2].reshape(queries.shape), results[3].reshape(queries.shape))
```

```python
import functools
import math

import jax
import jax.numpy as jnp
from jax import lax
from jax.experimental import pallas as pl
from jax.experimental.pallas import tpu as pltpu
from jax.sharding import PartitionSpec as P

F32 = jnp.float32
BF16 = jnp.bfloat16
AXES = ("col", "row")
BLOCK = 256
SMALL = 128


def contract(a, b, dim_a, dim_b):
    return lax.dot_general(
        a, b, (((dim_a,), (dim_b,)), ((), ())), preferred_element_type=F32
    )


def level_weights(table, profile_row, width):
    profiles, levels = table.shape
    places = lax.broadcasted_iota(jnp.int32, (profiles, profile_row.shape[1]), 0)
    onehot = jnp.where(places == profile_row, 1.0, 0.0).astype(BF16)
    high = table.astype(BF16)
    rest = table - high.astype(F32)
    middle = rest.astype(BF16)
    low = (rest - middle.astype(F32)).astype(BF16)
    picked = (contract(onehot, high, 0, 0) + contract(onehot, middle, 0, 0)) + contract(
        onehot, low, 0, 0
    )
    depth = lax.broadcasted_iota(jnp.int32, (1, levels), 1).astype(F32)
    return picked * (jnp.exp2(-0.5 * depth) / math.sqrt(width))


def weighted_stack(q, w, levels):
    q_wide = q.astype(F32)
    return jnp.concatenate([(q_wide * w[:, l : l + 1]).astype(BF16) for l in levels], axis=1)


def first_kernel(first_far, width, heads, ends, profile, table, q, k, v, g, w_out, s_out, g_out):
    for h in range(heads):
        lanes = slice(h * width, (h + 1) * width)
        w = level_weights(table[:, h, :], profile[...], width)
        w_out[h] = w
        s_out[h] = contract(k[:, lanes], v[:, lanes], 0, 0)
        stack = weighted_stack(q[:, lanes], w, [first_far + j for j in ends])
        states = contract(g[:, lanes], stack, 0, 0)
        for i in range(len(ends)):
            g_out[i, h] = states[:, i * width : (i + 1) * width]


def second_kernel(first_far, width, heads, middle, w_in, q, g, g_out):
    for h in range(heads):
        lanes = slice(h * width, (h + 1) * width)
        stack = weighted_stack(q[:, lanes], w_in[h], [first_far + j for j in middle])
        states = contract(g[:, lanes], stack, 0, 0)
        for i in range(len(middle)):
            g_out[i, h] = states[:, i * width : (i + 1) * width]


def block_mask(w, levels, causal):
    parts = []
    for i in range(BLOCK // SMALL):
        rows = w[i * SMALL : (i + 1) * SMALL]
        tri = jnp.broadcast_to(rows[:, 0:1], (SMALL, SMALL))
        for l in range(1, SMALL.bit_length()):
            tri = jnp.where(levels >= l, rows[:, l : l + 1], tri)
        line = []
        for j in range(BLOCK // SMALL):
            if j > i:
                line.append(jnp.zeros((SMALL, SMALL), F32))
            elif j == i:
                line.append(jnp.where(causal, tri, 0.0))
            else:
                l = SMALL.bit_length() - 1 + (i ^ j).bit_length()
                line.append(jnp.broadcast_to(rows[:, l : l + 1], (SMALL, SMALL)))
        parts.append(jnp.concatenate(line, axis=1))
    return jnp.concatenate(parts, axis=0)


def tile_kernel(w_in, q, k, v, g, out, dq, dk, dv):
    tokens = q.shape[0]
    places_t = lax.broadcasted_iota(jnp.int32, (SMALL, SMALL), 0)
    places_s = lax.broadcasted_iota(jnp.int32, (SMALL, SMALL), 1)
    differ = places_t ^ places_s
    levels = jnp.zeros((SMALL, SMALL), jnp.int32)
    for p in range(SMALL.bit_length() - 1):
        levels = levels + jnp.where(differ >= 1 << p, 1, 0)
    causal = places_s <= places_t
    for start in range(0, tokens, BLOCK):
        rows = slice(start, start + BLOCK)
        qb, kb, vb, gb = q[rows, :], k[rows, :], v[rows, :], g[rows, :]
        mask = block_mask(w_in[0, rows, :], levels, causal)
        probs = (contract(qb, kb, 1, 1) * mask).astype(BF16)
        grads = (contract(gb, vb, 1, 1) * mask).astype(BF16)
        out[rows, :] = contract(probs, vb, 1, 0)
        dq[rows, :] = contract(grads, kb, 1, 0)
        dk[rows, :] = contract(grads, qb, 0, 0)
        dv[rows, :] = contract(probs, gb, 0, 0)
    size = BLOCK
    while size < tokens:
        l = size.bit_length()
        for start in range(0, tokens, 2 * size):
            low = slice(start, start + size)
            up = slice(start + size, start + 2 * size)
            w = w_in[0, up, l : l + 1]
            state = contract(k[low, :], v[low, :], 0, 0).astype(BF16)
            out[up, :] = out[up, :] + w * contract(q[up, :], state, 1, 0)
            dq[up, :] = dq[up, :] + w * contract(g[up, :], state, 1, 1)
            weighted = (q[up, :].astype(F32) * w).astype(BF16)
            pulled = contract(g[up, :], weighted, 0, 0).astype(BF16)
            dk[low, :] = dk[low, :] + contract(v[low, :], pulled, 1, 0)
            dv[low, :] = dv[low, :] + contract(k[low, :], pulled, 1, 1)
        size *= 2


def far_sums(first, width, h, w_in, q, g, buckets, count):
    lanes = slice(h * width, (h + 1) * width)
    qh, gh = q[:, lanes], g[:, lanes]
    out = dq = None
    for i in range(count):
        state = buckets[i, h].astype(BF16)
        w = w_in[h, :, first + i : first + i + 1]
        o = w * contract(qh, state, 1, 0)
        d = w * contract(gh, state, 1, 1)
        out, dq = (o, d) if out is None else (out + o, dq + d)
    return out, dq


def far_kernel(first, width, heads, count, w_in, q, g, buckets, out, dq):
    for h in range(heads):
        lanes = slice(h * width, (h + 1) * width)
        out[:, lanes], dq[:, lanes] = far_sums(first, width, h, w_in, q, g, buckets, count)


def last_kernel(first, width, heads, count, w_in, q, k, v, g, buckets, pulled, far_out, far_dq, *refs):
    local, (out, dq, dk, dv) = refs[:-4], refs[-4:]
    for h in range(heads):
        lanes = slice(h * width, (h + 1) * width)
        o, d = far_sums(first, width, h, w_in, q, g, buckets, count)
        l_out, l_dq, l_dk, l_dv = local[4 * h : 4 * h + 4]
        state = pulled[h].astype(BF16)
        out[:, lanes] = l_out[...] + (far_out[:, lanes] + o)
        dq[:, lanes] = l_dq[...] + (far_dq[:, lanes] + d)
        dk[:, lanes] = l_dk[...] + contract(v[:, lanes], state, 1, 0)
        dv[:, lanes] = l_dv[...] + contract(k[:, lanes], state, 1, 1)


def links(row_bits, col_bits):
    steps = []
    place = 1
    while place < row_bits:
        steps.append(1 << place)
        if place + 1 < row_bits:
            steps.append(3 << place)
        place += 2
    for bit in range(col_bits):
        if bit == col_bits - 1 and bit > 0:
            steps.append(((1 << col_bits) - 1) << row_bits)
        else:
            steps.append(1 << row_bits + bit)
    return steps


def tie(*trees):
    return lax.optimization_barrier(trees)


def shards(row_size, col_size, queries, keys, values, out_grad, weight_table, profile):
    tokens, columns = queries.shape
    profiles, heads, depth = weight_table.shape
    width = columns // heads
    row_bits = row_size.bit_length() - 1
    col_bits = col_size.bit_length() - 1
    far = row_bits + col_bits
    first_far = tokens.bit_length()
    devices = row_size * col_size
    own = lax.axis_index("col") * row_size + lax.axis_index("row")
    core = own & 1
    on_first = core == 0
    profile_row = profile.reshape(1, tokens)

    def full(shape, kind=F32):
        return jax.ShapeDtypeStruct(shape, kind)

    square = (heads, width, width)
    ends = (far - 1, 0)
    middle = tuple(range(1, far - 1))
    unit = tokens * width * width * heads * 2
    weights, state, end_grads = pl.pallas_call(
        functools.partial(first_kernel, first_far, width, heads, ends),
        out_shape=(full((heads, tokens, depth)), full(square), full((2,) + square)),
        name="first",
        cost_estimate=pl.CostEstimate(
            flops=3 * unit, bytes_accessed=4 * tokens * columns * 2, transcendentals=0
        ),
    )(profile_row, weight_table, queries, keys, values, out_grad)

    exchange = [(i, i ^ 1) for i in range(devices)]
    hand_over = [(i, i ^ 1) for i in range(0, devices, 2)]
    payload = jnp.stack([state, jnp.where(on_first, end_grads[0], end_grads[1])])
    other = lax.ppermute(payload, AXES, exchange)
    middle_grads = pl.pallas_call(
        functools.partial(second_kernel, first_far, width, heads, middle),
        out_shape=full((len(middle),) + square),
        name="second",
        cost_estimate=pl.CostEstimate(
            flops=len(middle) * unit, bytes_accessed=tokens * columns * 4, transcendentals=0
        ),
    )(weights, queries, out_grad)
    other_middle = lax.ppermute(middle_grads, AXES, hand_over)

    steps = links(row_bits, col_bits)
    rounds = len(steps)
    carried = jnp.where(on_first, state + other[0], 0.0)
    received = []

    def tile_part(h):
        block = pl.BlockSpec((tokens, width), lambda i: (0, h))
        whole = pl.BlockSpec((tokens, width), lambda i: (0, 0))

        def run(w, q, k, v, g):
            return pl.pallas_call(
                tile_kernel,
                grid=(1,),
                in_specs=[pl.BlockSpec((1, tokens, depth), lambda i: (h, 0, 0))] + [block] * 4,
                out_specs=[whole] * 4,
                out_shape=[full((tokens, width))] * 4,
                name=f"tile{h}",
                cost_estimate=pl.CostEstimate(
                    flops=12 * tokens * BLOCK * width,
                    bytes_accessed=tokens * width * 24,
                    transcendentals=0,
                ),
            )(w, q, k, v, g)

        return run

    early = 5

    def early_far(w, q, g, buckets):
        return pl.pallas_call(
            functools.partial(far_kernel, first_far, width, heads, early),
            out_shape=[full((tokens, columns))] * 2,
            name="far",
            cost_estimate=pl.CostEstimate(
                flops=2 * early * unit, bytes_accessed=tokens * columns * 12, transcendentals=0
            ),
        )(w, q, g, buckets)

    local = {}
    for r in range(1, rounds + 1):
        level = far - r
        is_upper = (core == 1) & ((own >> level & 1) == 1)
        own_part = end_grads[0] if level == far - 1 else middle_grads[level - 1]
        from_other = other[1] if level == far - 1 else other_middle[level - 1]
        send = carried + jnp.where(is_upper, own_part + from_other, 0.0)
        pairs = [
            (i, i ^ (steps[rounds - r] if i & 1 else steps[r - 1])) for i in range(devices)
        ]
        work = None
        if r <= heads:
            work, operands = tile_part(r - 1), (weights, queries, keys, values, out_grad)
        if r == rounds - 1:
            taken = []
            for l in range(early):
                if l == 0:
                    here = jnp.where(on_first, 0.0, other[0])
                else:
                    here = jnp.where(on_first, received[l - 1], handed[l - 1])
                    here = jnp.where((own >> l & 1) == 1, here, 0.0)
                taken.append(here)
            work, operands = early_far, (weights, queries, out_grad, jnp.stack(taken))
        if work is not None:
            send, operands = tie(send, operands)
        got = lax.ppermute(send, AXES, pairs)
        if work is not None:
            result = work(*operands)
            got, result = tie(got, result)
            local[r] = result
        received.append(got)
        carried = carried + got
        if r == early - 1:
            handed = lax.ppermute(jnp.stack(received), AXES, hand_over)

    late = far - early
    payload = jnp.stack(
        [jnp.where(on_first, received[early - 1], carried)] + received[early:]
    )
    final = lax.ppermute(payload, AXES, exchange)
    buckets = []
    for i in range(late):
        here = jnp.where(on_first, received[early - 1 + i], final[i])
        buckets.append(jnp.where((own >> early + i & 1) == 1, here, 0.0))
    pulled = jnp.where(on_first, final[0] + other[1], carried)

    far_out, far_dq = local[rounds - 1]
    span = min(tokens, 256)
    wide = pl.BlockSpec((span, columns), lambda i: (i, 0))
    narrow = pl.BlockSpec((span, width), lambda i: (i, 0))
    return pl.pallas_call(
        functools.partial(last_kernel, first_far + early, width, heads, late),
        grid=(tokens // span,),
        in_specs=[pl.BlockSpec((heads, span, depth), lambda i: (0, i, 0))]
        + [wide] * 4
        + [
            pl.BlockSpec((late,) + square, lambda i: (0, 0, 0, 0)),
            pl.BlockSpec(square, lambda i: (0, 0, 0)),
        ]
        + [wide] * 2
        + [narrow] * (4 * heads),
        out_specs=[wide] * 4,
        out_shape=[full((tokens, columns))] * 4,
        name="last",
        cost_estimate=pl.CostEstimate(
            flops=(2 * late + 2) * unit, bytes_accessed=tokens * columns * 40, transcendentals=0
        ),
    )(
        weights,
        queries,
        keys,
        values,
        out_grad,
        jnp.stack(buckets),
        pulled,
        far_out,
        far_dq,
        *[part for h in range(heads) for part in local[h + 1]],
    )


def solution(mesh):
    spread = P(AXES, None)
    body = functools.partial(shards, mesh.shape["row"], mesh.shape["col"])
    return jax.shard_map(
        body,
        mesh=mesh,
        in_specs=(spread,) * 4 + (P(), P(AXES)),
        out_specs=(spread,) * 4,
        check_vma=False,
    )
```

```python
import functools
import math

import jax
import jax.numpy as jnp
from jax import lax
from jax.experimental import pallas as pl
from jax.experimental.pallas import tpu as pltpu
from jax.sharding import PartitionSpec as P

F32 = jnp.float32
BF16 = jnp.bfloat16
AXES = ("col", "row")
BLOCK = 256
SMALL = 128
STRIDE = 64
ROOM = 16 << 20
VMEM = pl.BlockSpec(memory_space=pltpu.VMEM)


def contract(a, b, dim_a, dim_b):
    return lax.dot_general(
        a, b, (((dim_a,), (dim_b,)), ((), ())), preferred_element_type=F32
    )


def call(kernel, name, out_shape, flops, moved, **rest):
    return pl.pallas_call(
        kernel,
        out_shape=out_shape,
        name=name,
        cost_estimate=pl.CostEstimate(flops=flops, bytes_accessed=moved, transcendentals=0),
        compiler_params=pltpu.CompilerParams(vmem_limit_bytes=ROOM),
        **rest,
    )


def level_weights(table, profile_row, width):
    levels, heads, profiles = table.shape
    places = lax.broadcasted_iota(jnp.int32, (profiles, profile_row.shape[1]), 0)
    onehot = jnp.where(places == profile_row, 1.0, 0.0).astype(BF16)
    blank = jnp.zeros((STRIDE - levels, profiles), F32)
    rows = []
    for h in range(heads):
        rows += [table[:, h, :], blank]
    rows = jnp.concatenate(rows, axis=0)
    high = rows.astype(BF16)
    rest = rows - high.astype(F32)
    middle = rest.astype(BF16)
    low = (rest - middle.astype(F32)).astype(BF16)
    picked = (contract(onehot, high, 0, 1) + contract(onehot, middle, 0, 1)) + contract(
        onehot, low, 0, 1
    )
    depth = (lax.broadcasted_iota(jnp.int32, (1, heads * STRIDE), 1) & (STRIDE - 1)).astype(F32)
    return picked * (jnp.exp2(-0.5 * depth) / math.sqrt(width))


def weighted(x, w, h, level):
    at = h * STRIDE + level
    return (x.astype(F32) * w[:, at : at + 1]).astype(BF16)


def first_kernel(top, width, heads, profile, table, q, k, v, g, w_out, ends_out):
    w = level_weights(table, profile[...], width)
    w_out[...] = w
    for h in range(heads):
        lanes = slice(h * width, (h + 1) * width)
        ends_out[0, h] = contract(k[:, lanes], v[:, lanes], 0, 0)
        ends_out[1, h] = contract(g[:, lanes], weighted(q[:, lanes], w, h, top), 0, 0)


def second_kernel(first_far, width, heads, far, w, q, g, low_out, middle_out):
    for h in range(heads):
        lanes = slice(h * width, (h + 1) * width)
        stack = [weighted(q[:, lanes], w, h, first_far + j) for j in range(far - 1)]
        states = contract(g[:, lanes], jnp.concatenate(stack, axis=1), 0, 0)
        low_out[h] = states[:, :width]
        for j in range(1, far - 1):
            middle_out[j - 1, h] = states[:, j * width : (j + 1) * width]


def block_mask(w, levels, causal):
    parts = []
    for i in range(BLOCK // SMALL):
        rows = w[i * SMALL : (i + 1) * SMALL]
        tri = jnp.broadcast_to(rows[:, 0:1], (SMALL, SMALL))
        for l in range(1, SMALL.bit_length()):
            tri = jnp.where(levels >= l, rows[:, l : l + 1], tri)
        line = []
        for j in range(BLOCK // SMALL):
            if j > i:
                line.append(jnp.zeros((SMALL, SMALL), F32))
            elif j == i:
                line.append(jnp.where(causal, tri, 0.0))
            else:
                l = SMALL.bit_length() - 1 + (i ^ j).bit_length()
                line.append(jnp.broadcast_to(rows[:, l : l + 1], (SMALL, SMALL)))
        parts.append(jnp.concatenate(line, axis=1))
    return jnp.concatenate(parts, axis=0)


def tile_kernel(i, width, heads, depth, first_far, place, w, q, k, v, g, ends, out, dq, dk, dv):
    tokens = q.shape[0]
    on_first = (place[0] & 1) == 0
    places_t = lax.broadcasted_iota(jnp.int32, (SMALL, SMALL), 0)
    places_s = lax.broadcasted_iota(jnp.int32, (SMALL, SMALL), 1)
    differ = places_t ^ places_s
    levels = jnp.zeros((SMALL, SMALL), jnp.int32)
    for p in range(SMALL.bit_length() - 1):
        levels = levels + jnp.where(differ >= 1 << p, 1, 0)
    causal = places_s <= places_t
    rows = slice(i * BLOCK, (i + 1) * BLOCK)
    for h in range(heads):
        lanes = slice(h * width, (h + 1) * width)
        first = h * STRIDE
        qb, kb, vb, gb = q[rows, lanes], k[rows, lanes], v[rows, lanes], g[rows, lanes]
        mask = block_mask(w[rows, first : first + depth], levels, causal)
        probs = (contract(qb, kb, 1, 1) * mask).astype(BF16)
        grads = (contract(gb, vb, 1, 1) * mask).astype(BF16)
        state = jnp.where(on_first, 0.0, ends[0, h]).astype(BF16)
        scale = w[rows, first + first_far : first + first_far + 1]
        o = contract(probs, vb, 1, 0) + scale * contract(qb, state, 1, 0)
        d = contract(grads, kb, 1, 0) + scale * contract(gb, state, 1, 1)
        s = contract(grads, qb, 0, 0)
        e = contract(probs, gb, 0, 0)
        size = BLOCK
        while size < tokens:
            group = i * BLOCK // size
            sibling = slice((group ^ 1) * size, ((group ^ 1) + 1) * size)
            at = first + size.bit_length()
            if group & 1:
                scale = w[rows, at : at + 1]
                state = contract(k[sibling, lanes], v[sibling, lanes], 0, 0).astype(BF16)
                o = o + scale * contract(qb, state, 1, 0)
                d = d + scale * contract(gb, state, 1, 1)
            else:
                scaled = (q[sibling, lanes].astype(F32) * w[sibling, at : at + 1]).astype(BF16)
                pulled = contract(g[sibling, lanes], scaled, 0, 0).astype(BF16)
                s = s + contract(vb, pulled, 1, 0)
                e = e + contract(kb, pulled, 1, 1)
            size *= 2
        out[:, lanes] = o
        dq[:, lanes] = d
        dk[:, lanes] = s
        dv[:, lanes] = e


def last_kernel(
    width, heads, far, first_far, place, w, q, k, v, g, stacked, alone, top, handed, alone_in, final,
    carried, *refs,
):
    own = place[0]
    on_first = (own & 1) == 0
    local, (out, dq, dk, dv, tall, broad, pulled, near, arrived) = refs[:-9], refs[-9:]
    step = pl.program_id(0)
    fetches = [pltpu.make_async_copy(part, near.at[n], arrived.at[n]) for n, part in enumerate(local)]

    @pl.when(step == 0)
    def _():
        for fetch in fetches:
            fetch.start()
        for h in range(heads):
            for j in range(1, far):
                if j < far - 2:
                    state = jnp.where(on_first, stacked[j - 1, h], handed[j - 1, h])
                elif j == far - 2:
                    state = jnp.where(on_first, alone[h], alone_in[h])
                else:
                    state = jnp.where(on_first, top[h], final[h])
                half = jnp.where((own >> j & 1) == 1, state, 0.0).astype(BF16)
                tall[h, (j - 1) * width : j * width, :] = half
                broad[h, :, (j - 1) * width : j * width] = half
            pulled[h] = jnp.where(on_first, final[h], carried[h]).astype(BF16)

    for i in range(q.shape[0] // BLOCK):

        @pl.when(step == i)
        def _(i=i):
            rows = slice(i * BLOCK, (i + 1) * BLOCK)
            for fetch in fetches[4 * i : 4 * i + 4]:
                fetch.wait()
            l_out, l_dq, l_dk, l_dv = (near.at[4 * i + n] for n in range(4))
            for h in range(heads):
                lanes = slice(h * width, (h + 1) * width)
                scaled_q = [weighted(q[rows, lanes], w[rows, :], h, first_far + j) for j in range(1, far)]
                scaled_g = [weighted(g[rows, lanes], w[rows, :], h, first_far + j) for j in range(1, far)]
                o = contract(jnp.concatenate(scaled_q, axis=1), tall[h], 1, 0)
                d = contract(jnp.concatenate(scaled_g, axis=1), broad[h], 1, 1)
                out[:, lanes] = l_out[:, lanes] + o
                dq[:, lanes] = l_dq[:, lanes] + d
                dk[:, lanes] = l_dk[:, lanes] + contract(v[rows, lanes], pulled[h], 1, 0)
                dv[:, lanes] = l_dv[:, lanes] + contract(k[rows, lanes], pulled[h], 1, 1)


def links(row_bits, col_bits):
    steps = []
    place = 1
    while place < row_bits:
        steps.append(1 << place)
        if place + 1 < row_bits:
            steps.append(3 << place)
        place += 2
    for bit in range(col_bits):
        if bit == col_bits - 1 and bit > 0:
            steps.append(((1 << col_bits) - 1) << row_bits)
        else:
            steps.append(1 << row_bits + bit)
    return steps


def tie(*trees):
    return lax.optimization_barrier(trees)


def shards(row_size, col_size, queries, keys, values, out_grad, weight_table, profile):
    tokens, columns = queries.shape
    profiles, heads, depth = weight_table.shape
    width = columns // heads
    row_bits = row_size.bit_length() - 1
    col_bits = col_size.bit_length() - 1
    far = row_bits + col_bits
    first_far = tokens.bit_length()
    devices = row_size * col_size
    own = lax.axis_index("col") * row_size + lax.axis_index("row")
    core = own & 1
    on_first = core == 0
    profile_row = profile.reshape(1, tokens)
    table = jnp.transpose(weight_table, (2, 1, 0))

    def full(shape, kind=F32):
        return jax.ShapeDtypeStruct(shape, kind)

    square = (heads, width, width)
    unit = tokens * width * width * heads * 2
    array = tokens * columns * 2
    exchange = [(i, i ^ 1) for i in range(devices)]
    hand_over = [(i, i ^ 1) for i in range(0, devices, 2)]

    weights, ends = call(
        functools.partial(first_kernel, first_far + far - 1, width, heads),
        "first",
        (full((tokens, heads * STRIDE)), full((2,) + square)),
        3 * unit,
        4 * array,
        in_specs=[VMEM] * 6,
        out_specs=[VMEM] * 2,
    )(profile_row, table, queries, keys, values, out_grad)
    other = lax.ppermute(ends, AXES, exchange)

    def second(w, q, g):
        return call(
            functools.partial(second_kernel, first_far, width, heads, far),
            "second",
            (full(square), full((far - 2,) + square)),
            far * unit,
            4 * array,
            in_specs=[VMEM] * 3,
            out_specs=[VMEM] * 2,
        )(w, q, g)

    smem = pl.BlockSpec(memory_space=pltpu.SMEM)
    place = own.reshape(1).astype(jnp.int32)
    blocks = tokens // BLOCK

    def tile(i, *operands):
        return call(
            functools.partial(tile_kernel, i, width, heads, depth, first_far),
            f"tile{i}",
            [full((BLOCK, columns))] * 4,
            20 * BLOCK * BLOCK * columns,
            6 * array,
            in_specs=[smem] + [VMEM] * 6,
            out_specs=[VMEM] * 4,
        )(place, *operands)

    steps = links(row_bits, col_bits)
    rounds = len(steps)
    carried = jnp.where(on_first, ends[0] + other[0], 0.0)
    received = []
    local = []
    for r in range(1, rounds + 1):
        level = far - r
        is_upper = (core == 1) & ((own >> level & 1) == 1)
        if r == 1:
            own_part, from_other = ends[1], other[1]
        else:
            own_part, from_other = middle[level - 1], other_middle[level - 1]
        send = carried + jnp.where(is_upper, own_part + from_other, 0.0)
        pairs = [
            (i, i ^ (steps[rounds - r] if i & 1 else steps[r - 1])) for i in range(devices)
        ]
        work, operands = None, ()
        if r == 1:
            work, operands = second, (weights, queries, out_grad)
        elif r - 2 < blocks:
            work = functools.partial(tile, r - 2)
            operands = (weights, queries, keys, values, out_grad, other)
        elif r == rounds - 1:
            work, operands = (lambda *parts: jnp.stack(parts)), tuple(received)
        send, operands = tie(send, operands)
        got = lax.ppermute(send, AXES, pairs)
        if r == rounds:
            handed = lax.ppermute(stacked, AXES, hand_over)
            alone = received[-1]
            alone_in = lax.ppermute(alone, AXES, hand_over)
            got, handed, alone_in = tie(got, handed, alone_in)
        elif r == 1:
            low_grads, middle = work(*operands)
            other_middle = lax.ppermute(middle, AXES, hand_over)
            got, low_grads, middle = tie(got, low_grads, middle)
        else:
            result = work(*operands)
            got, result = tie(got, result)
            if r == rounds - 1:
                stacked = result
            else:
                local += list(result)
        received.append(got)
        carried = carried + got

    top = received[-1]
    final = lax.ppermute(jnp.where(on_first, top, carried + low_grads), AXES, exchange)

    wide = pl.BlockSpec((BLOCK, columns), lambda i: (i, 0))
    return call(
        functools.partial(last_kernel, width, heads, far, first_far),
        "last",
        [full((tokens, columns))] * 4,
        (2 * far + 2) * unit,
        16 * array,
        grid=(blocks,),
        in_specs=[smem] + [VMEM] * 12 + [pl.BlockSpec(memory_space=pl.ANY)] * len(local),
        out_specs=[wide] * 4,
        scratch_shapes=[
            pltpu.VMEM((heads, (far - 1) * width, width), BF16),
            pltpu.VMEM((heads, width, (far - 1) * width), BF16),
            pltpu.VMEM(square, BF16),
            pltpu.VMEM((len(local), BLOCK, columns), F32),
            pltpu.SemaphoreType.DMA((len(local),)),
        ],
    )(
        place, weights, queries, keys, values, out_grad, stacked, alone, top, handed, alone_in, final,
        carried, *local,
    )


def solution(mesh):
    spread = P(AXES, None)
    body = functools.partial(shards, mesh.shape["row"], mesh.shape["col"])
    return jax.shard_map(
        body,
        mesh=mesh,
        in_specs=(spread,) * 4 + (P(), P(AXES)),
        out_specs=(spread,) * 4,
        check_vma=False,
    )
```

```python
import functools
import math

import jax
import jax.numpy as jnp
from jax import lax
from jax.experimental import pallas as pl
from jax.experimental.pallas import tpu as pltpu
from jax.sharding import PartitionSpec as P


F32 = jnp.float32
BF16 = jnp.bfloat16
AXES = ("col", "row")
BLOCK = 256
SMALL = 128
STRIDE = 64
ROOM = 16 << 20
VMEM = pl.BlockSpec(memory_space=pltpu.VMEM)
HBM = pl.BlockSpec(memory_space=pltpu.HBM)


def contract(a, b, dim_a, dim_b):
    return lax.dot_general(
        a, b, (((dim_a,), (dim_b,)), ((), ())), preferred_element_type=F32
    )


def outside(*arrays):
    return [pltpu.with_memory_space_constraint(x, pltpu.HBM) for x in arrays]


def call(kernel, out_shape, flops, moved, **rest):
    return pl.pallas_call(
        kernel,
        out_shape=out_shape,
        cost_estimate=pl.CostEstimate(flops=flops, bytes_accessed=moved, transcendentals=0),
        compiler_params=pltpu.CompilerParams(vmem_limit_bytes=ROOM),
        **rest,
    )


def level_weights(table, profile_row, width):
    levels, heads, profiles = table.shape
    places = lax.broadcasted_iota(jnp.int32, (profiles, profile_row.shape[1]), 0)
    onehot = jnp.where(places == profile_row, 1.0, 0.0).astype(BF16)
    blank = jnp.zeros((STRIDE - levels, profiles), F32)
    rows = []
    for h in range(heads):
        rows += [table[:, h, :], blank]
    rows = jnp.concatenate(rows, axis=0)
    high = rows.astype(BF16)
    rest = rows - high.astype(F32)
    middle = rest.astype(BF16)
    low = (rest - middle.astype(F32)).astype(BF16)
    picked = (contract(onehot, high, 0, 1) + contract(onehot, middle, 0, 1)) + contract(
        onehot, low, 0, 1
    )
    depth = (lax.broadcasted_iota(jnp.int32, (1, heads * STRIDE), 1) & (STRIDE - 1)).astype(F32)
    return picked * (jnp.exp2(-0.5 * depth) / math.sqrt(width))


def weighted(x, w, h, level):
    at = h * STRIDE + level
    return (x.astype(F32) * w[:, at : at + 1]).astype(BF16)


def first_kernel(
    top, width, heads, profile_in, table_in, q_in, k_in, v_in, g_in, w_out, ends_out,
    profile, table, q, k, v, g, arrived,
):
    fetches = [
        pltpu.make_async_copy(source, target, arrived.at[n])
        for n, (source, target) in enumerate(
            (
                (profile_in, profile),
                (table_in, table),
                (k_in, k),
                (v_in, v),
                (q_in, q),
                (g_in, g),
            )
        )
    ]
    for fetch in fetches:
        fetch.start()
    fetches[0].wait()
    fetches[1].wait()
    w = level_weights(table, profile[...], width)
    w_out[...] = w
    fetches[2].wait()
    fetches[3].wait()
    for h in range(heads):
        lanes = slice(h * width, (h + 1) * width)
        ends_out[0, h] = contract(k[:, lanes], v[:, lanes], 0, 0)
    fetches[4].wait()
    fetches[5].wait()
    for h in range(heads):
        lanes = slice(h * width, (h + 1) * width)
        ends_out[1, h] = contract(g[:, lanes], weighted(q[:, lanes], w, h, top), 0, 0)


def second_kernel(first_far, width, heads, far, w, q, g, low_out, middle_out):
    for h in range(heads):
        lanes = slice(h * width, (h + 1) * width)
        stack = [weighted(q[:, lanes], w, h, first_far + j) for j in range(far - 1)]
        states = contract(g[:, lanes], jnp.concatenate(stack, axis=1), 0, 0)
        low_out[h] = states[:, :width]
        for j in range(1, far - 1):
            middle_out[j - 1, h] = states[:, j * width : (j + 1) * width]


def block_mask(w, levels, causal):
    parts = []
    for i in range(BLOCK // SMALL):
        rows = w[i * SMALL : (i + 1) * SMALL]
        tri = jnp.broadcast_to(rows[:, 0:1], (SMALL, SMALL))
        for l in range(1, SMALL.bit_length()):
            tri = jnp.where(levels >= l, rows[:, l : l + 1], tri)
        line = []
        for j in range(BLOCK // SMALL):
            if j > i:
                line.append(jnp.zeros((SMALL, SMALL), F32))
            elif j == i:
                line.append(jnp.where(causal, tri, 0.0))
            else:
                l = SMALL.bit_length() - 1 + (i ^ j).bit_length()
                line.append(jnp.broadcast_to(rows[:, l : l + 1], (SMALL, SMALL)))
        parts.append(jnp.concatenate(line, axis=1))
    return jnp.concatenate(parts, axis=0)


def merge_kernel(count, place, own_part, from_other, *sums):
    own = place[0]
    for l in range(count):
        taken = ((own & 1) == 1) & ((own >> l + 1 & 1) == 1)
        sums[l][...] = jnp.where(taken, own_part[l] + from_other[l], 0.0)


def tile_kernel(i, width, heads, depth, first_far, place, w, q, k, v, g, ends, out, dq, dk, dv):
    tokens = q.shape[0]
    on_first = (place[0] & 1) == 0
    places_t = lax.broadcasted_iota(jnp.int32, (SMALL, SMALL), 0)
    places_s = lax.broadcasted_iota(jnp.int32, (SMALL, SMALL), 1)
    differ = places_t ^ places_s
    levels = jnp.zeros((SMALL, SMALL), jnp.int32)
    for p in range(SMALL.bit_length() - 1):
        levels = levels + jnp.where(differ >= 1 << p, 1, 0)
    causal = places_s <= places_t
    rows = slice(i * BLOCK, (i + 1) * BLOCK)
    for h in range(heads):
        lanes = slice(h * width, (h + 1) * width)
        first = h * STRIDE
        qb, kb, vb, gb = q[rows, lanes], k[rows, lanes], v[rows, lanes], g[rows, lanes]
        mask = block_mask(w[rows, first : first + depth], levels, causal)
        probs = (contract(qb, kb, 1, 1) * mask).astype(BF16)
        grads = (contract(gb, vb, 1, 1) * mask).astype(BF16)
        state = jnp.where(on_first, 0.0, ends[0, h]).astype(BF16)
        scale = w[rows, first + first_far : first + first_far + 1]
        o = contract(probs, vb, 1, 0) + scale * contract(qb, state, 1, 0)
        d = contract(grads, kb, 1, 0) + scale * contract(gb, state, 1, 1)
        s = contract(grads, qb, 0, 0)
        e = contract(probs, gb, 0, 0)
        size = BLOCK
        while size < tokens:
            group = i * BLOCK // size
            sibling = slice((group ^ 1) * size, ((group ^ 1) + 1) * size)
            at = first + size.bit_length()
            if group & 1:
                scale = w[rows, at : at + 1]
                state = contract(k[sibling, lanes], v[sibling, lanes], 0, 0).astype(BF16)
                o = o + scale * contract(qb, state, 1, 0)
                d = d + scale * contract(gb, state, 1, 1)
            else:
                scaled = (q[sibling, lanes].astype(F32) * w[sibling, at : at + 1]).astype(BF16)
                pulled = contract(g[sibling, lanes], scaled, 0, 0).astype(BF16)
                s = s + contract(vb, pulled, 1, 0)
                e = e + contract(kb, pulled, 1, 1)
            size *= 2
        out[:, lanes] = o
        dq[:, lanes] = d
        dk[:, lanes] = s
        dv[:, lanes] = e


def far_kernel(
    width, heads, count, first_far, place, w, q, g, stacked, handed, *refs
):
    own = place[0]
    on_first = (own & 1) == 0
    local, (out, dq, near, arrived) = refs[:-4], refs[-4:]
    fetches = [pltpu.make_async_copy(part, near.at[n], arrived.at[n]) for n, part in enumerate(local)]
    for fetch in fetches:
        fetch.start()
    states = []
    for h in range(heads):
        of_head = []
        for j in range(1, count + 1):
            state = jnp.where(on_first, stacked[j - 1, h], handed[j - 1, h])
            of_head.append(jnp.where((own >> j & 1) == 1, state, 0.0).astype(BF16))
        states.append((jnp.concatenate(of_head, axis=0), jnp.concatenate(of_head, axis=1)))
    for i in range(q.shape[0] // BLOCK):
        rows = slice(i * BLOCK, (i + 1) * BLOCK)
        fetches[2 * i].wait()
        fetches[2 * i + 1].wait()
        for h in range(heads):
            lanes = slice(h * width, (h + 1) * width)
            scaled_q = [weighted(q[rows, lanes], w[rows, :], h, first_far + j) for j in range(1, count + 1)]
            scaled_g = [weighted(g[rows, lanes], w[rows, :], h, first_far + j) for j in range(1, count + 1)]
            tall, broad = states[h]
            o = contract(jnp.concatenate(scaled_q, axis=1), tall, 1, 0)
            d = contract(jnp.concatenate(scaled_g, axis=1), broad, 1, 1)
            out[rows, lanes] = near[2 * i, :, lanes] + o
            dq[rows, lanes] = near[2 * i + 1, :, lanes] + d


def last_kernel(
    width, heads, far, first_far, place, w, q, k, v, g, alone, top, alone_in, final, carried,
    far_out, far_dq, *refs,
):
    own = place[0]
    on_first = (own & 1) == 0
    local, (out, dq, dk, dv, near, arrived) = refs[:-6], refs[-6:]
    step = pl.program_id(0)
    fetches = [pltpu.make_async_copy(part, near.at[n], arrived.at[n]) for n, part in enumerate(local)]

    @pl.when(step == 0)
    def _():
        for fetch in fetches:
            fetch.start()

    for i in range(q.shape[0] // BLOCK):

        @pl.when(step == i)
        def _(i=i):
            rows = slice(i * BLOCK, (i + 1) * BLOCK)
            sums = []
            for h in range(heads):
                lanes = slice(h * width, (h + 1) * width)
                pair = []
                for j, here, there in ((far - 2, alone, alone_in), (far - 1, top, final)):
                    state = jnp.where(on_first, here[h], there[h])
                    pair.append(jnp.where((own >> j & 1) == 1, state, 0.0).astype(BF16))
                pulled = jnp.where(on_first, final[h], carried[h]).astype(BF16)
                scaled_q = [weighted(q[rows, lanes], w[rows, :], h, first_far + j) for j in (far - 2, far - 1)]
                scaled_g = [weighted(g[rows, lanes], w[rows, :], h, first_far + j) for j in (far - 2, far - 1)]
                o = contract(jnp.concatenate(scaled_q, axis=1), jnp.concatenate(pair, axis=0), 1, 0)
                d = contract(jnp.concatenate(scaled_g, axis=1), jnp.concatenate(pair, axis=1), 1, 1)
                out[:, lanes] = far_out[rows, lanes] + o
                dq[:, lanes] = far_dq[rows, lanes] + d
                sums.append((contract(v[rows, lanes], pulled, 1, 0), contract(k[rows, lanes], pulled, 1, 1)))
            fetches[2 * i].wait()
            fetches[2 * i + 1].wait()
            for h in range(heads):
                lanes = slice(h * width, (h + 1) * width)
                dk[:, lanes] = near[2 * i, :, lanes] + sums[h][0]
                dv[:, lanes] = near[2 * i + 1, :, lanes] + sums[h][1]


def links(row_bits, col_bits):
    steps = []
    place = 1
    while place < row_bits:
        steps.append(1 << place)
        if place + 1 < row_bits:
            steps.append(3 << place)
        place += 2
    for bit in range(col_bits):
        if bit == col_bits - 1 and bit > 0:
            steps.append(((1 << col_bits) - 1) << row_bits)
        else:
            steps.append(1 << row_bits + bit)
    return steps


def tie(*trees):
    return lax.optimization_barrier(trees)


def shards(row_size, col_size, queries, keys, values, out_grad, weight_table, profile):
    tokens, columns = queries.shape
    _, heads, depth = weight_table.shape
    width = columns // heads
    row_bits = row_size.bit_length() - 1
    col_bits = col_size.bit_length() - 1
    far = row_bits + col_bits
    first_far = tokens.bit_length()
    devices = row_size * col_size
    own = lax.axis_index("col") * row_size + lax.axis_index("row")
    core = own & 1
    on_first = core == 0
    profile_row = profile.reshape(1, tokens)
    table = jnp.transpose(weight_table, (2, 1, 0))

    def full(shape, kind=F32):
        return jax.ShapeDtypeStruct(shape, kind)

    square = (heads, width, width)
    unit = tokens * width * width * heads * 2
    array = tokens * columns * 2
    exchange = [(i, i ^ 1) for i in range(devices)]

    weights, ends = call(
        functools.partial(first_kernel, first_far + far - 1, width, heads),
        (full((tokens, heads * STRIDE)), full((2,) + square)),
        3 * unit,
        4 * array,
        in_specs=[HBM] * 6,
        out_specs=[VMEM] * 2,
        scratch_shapes=[
            pltpu.VMEM(profile_row.shape, jnp.int32),
            pltpu.VMEM(table.shape, F32),
        ]
        + [pltpu.VMEM((tokens, columns), BF16)] * 4
        + [pltpu.SemaphoreType.DMA((6,))],
    )(*outside(profile_row, table, queries, keys, values, out_grad))
    other = lax.ppermute(ends, AXES, exchange)

    def second(w, q, g):
        return call(
            functools.partial(second_kernel, first_far, width, heads, far),
            (full(square), full((far - 2,) + square)),
            far * unit,
            4 * array,
            in_specs=[VMEM] * 3,
        )(w, q, g)

    smem = pl.BlockSpec(memory_space=pltpu.SMEM)
    place = own.reshape(1).astype(jnp.int32)
    blocks = tokens // BLOCK

    def tile(i, *operands):
        return call(
            functools.partial(tile_kernel, i, width, heads, depth, first_far),
            [full((BLOCK, columns))] * 4,
            20 * BLOCK * BLOCK * columns,
            6 * array,
            in_specs=[smem] + [VMEM] * 5 + [pl.BlockSpec()],
        )(place, *operands)

    low_grads, middle = second(weights, queries, out_grad)
    other_middle = lax.ppermute(middle, AXES, exchange)

    def merge(own_part, from_other):
        return call(
            functools.partial(merge_kernel, far - 2),
            [full(square)] * (far - 2),
            far * width * width,
            array,
            in_specs=[smem] + [pl.BlockSpec()] * 2,
            out_specs=[VMEM] * (far - 2),
        )(place, own_part, from_other)

    steps = links(row_bits, col_bits)
    rounds = len(steps)
    carried = jnp.where(on_first, ends[0] + other[0], 0.0)
    received = []
    local = []
    for r in range(1, rounds + 1):
        if r == 1:
            is_upper = (core == 1) & ((own >> far - 1 & 1) == 1)
            send = carried + jnp.where(is_upper, ends[1] + other[1], 0.0)
            carried, send = tie(carried, send)
        else:
            send = carried + sums[far - r - 1]
        pairs = [
            (i, i ^ (steps[rounds - r] if i & 1 else steps[r - 1])) for i in range(devices)
        ]
        work, operands = None, ()
        if r == 1:
            work, operands = merge, (middle, other_middle)
        elif r - 2 < blocks:
            work = functools.partial(tile, r - 2)
            operands = (weights, queries, keys, values, out_grad, other)
        elif r == rounds - 1:
            work, operands = (lambda *parts: jnp.stack(parts)), tuple(received)
        if r > 1:
            send, operands = tie(send, operands)
        got = lax.ppermute(send, AXES, pairs)
        if r == rounds:
            alone = received[-1]
            alone_in = lax.ppermute(alone, AXES, exchange)
            firsts = outside(*[part for i in range(blocks) for part in local[4 * i : 4 * i + 2]])
            far_out, far_dq = call(
                functools.partial(far_kernel, width, heads, far - 3, first_far),
                [full((tokens, columns))] * 2,
                2 * (far - 3) * unit,
                8 * array,
                in_specs=[smem] + [VMEM] * 3 + [pl.BlockSpec()] * 2 + [HBM] * len(firsts),
                out_specs=[VMEM] * 2,
                scratch_shapes=[
                    pltpu.VMEM((len(firsts), BLOCK, columns), F32),
                    pltpu.SemaphoreType.DMA((len(firsts),)),
                ],
            )(place, weights, queries, out_grad, stacked, handed, *firsts)
            got, alone_in, far_out, far_dq = tie(got, alone_in, far_out, far_dq)
        elif r == 1:
            sums = work(*operands)
            got, sums = tie(got, sums)
        else:
            result = work(*operands)
            if r == rounds - 1:
                handed = lax.ppermute(result, AXES, exchange)
            got, result = tie(got, result)
            if r == rounds - 1:
                stacked = result
            else:
                local += list(result)
        received.append(got)
        carried = carried + got

    top = received[-1]
    final = lax.ppermute(jnp.where(on_first, top, carried + low_grads), AXES, exchange)

    wide = pl.BlockSpec((BLOCK, columns), lambda i: (i, 0))
    seconds = outside(*[part for i in range(blocks) for part in local[4 * i + 2 : 4 * i + 4]])
    return call(
        functools.partial(last_kernel, width, heads, far, first_far),
        [full((tokens, columns))] * 4,
        6 * unit,
        16 * array,
        grid=(blocks,),
        in_specs=[smem] + [VMEM] * 5 + [pl.BlockSpec()] * 5 + [VMEM] * 2 + [HBM] * len(seconds),
        out_specs=[wide] * 4,
        scratch_shapes=[
            pltpu.VMEM((len(seconds), BLOCK, columns), F32),
            pltpu.SemaphoreType.DMA((len(seconds),)),
        ],
    )(
        place, weights, queries, keys, values, out_grad, alone, top, alone_in, final, carried,
        far_out, far_dq, *seconds,
    )


def solution(mesh):
    spread = P(AXES, None)

    def body(*args):
        return shards(mesh.shape["row"], mesh.shape["col"], *args)

    return jax.shard_map(
        body,
        mesh=mesh,
        in_specs=(spread,) * 4 + (P(), P(AXES)),
        out_specs=(spread,) * 4,
        check_vma=False,
    )
```

```python
import functools
import math

import jax
import jax.numpy as jnp
from jax import lax
from jax.experimental import pallas as pl
from jax.experimental.pallas import tpu as pltpu
from jax.sharding import PartitionSpec as P


F32 = jnp.float32
BF16 = jnp.bfloat16
AXES = ("col", "row")
BLOCK = 256
SMALL = 128
STRIDE = 64
ROOM = 16 << 20
VMEM = pl.BlockSpec(memory_space=pltpu.VMEM)
HBM = pl.BlockSpec(memory_space=pltpu.HBM)


def contract(a, b, dim_a, dim_b):
    return lax.dot_general(
        a, b, (((dim_a,), (dim_b,)), ((), ())), preferred_element_type=F32
    )


def outside(*arrays):
    return [pltpu.with_memory_space_constraint(x, pltpu.HBM) for x in arrays]


def call(kernel, out_shape, flops, moved, **rest):
    return pl.pallas_call(
        kernel,
        out_shape=out_shape,
        cost_estimate=pl.CostEstimate(flops=flops, bytes_accessed=moved, transcendentals=0),
        compiler_params=pltpu.CompilerParams(vmem_limit_bytes=ROOM),
        **rest,
    )


def level_weights(table, profile_row, width):
    levels, heads, profiles = table.shape
    places = lax.broadcasted_iota(jnp.int32, (profiles, profile_row.shape[1]), 0)
    onehot = jnp.where(places == profile_row, 1.0, 0.0).astype(BF16)
    blank = jnp.zeros((STRIDE - levels, profiles), F32)
    rows = []
    for h in range(heads):
        rows += [table[:, h, :], blank]
    rows = jnp.concatenate(rows, axis=0)
    high = rows.astype(BF16)
    rest = rows - high.astype(F32)
    middle = rest.astype(BF16)
    low = (rest - middle.astype(F32)).astype(BF16)
    picked = (contract(onehot, high, 0, 1) + contract(onehot, middle, 0, 1)) + contract(
        onehot, low, 0, 1
    )
    depth = (lax.broadcasted_iota(jnp.int32, (1, heads * STRIDE), 1) & (STRIDE - 1)).astype(F32)
    return picked * (jnp.exp2(-0.5 * depth) / math.sqrt(width))


def weighted(x, w, h, level):
    at = h * STRIDE + level
    return (x.astype(F32) * w[:, at : at + 1]).astype(BF16)


def first_kernel(
    top, width, heads, profile_in, table_in, q_in, k_in, v_in, g_in, w_out, ends_out,
    profile, table, q, k, v, g, arrived,
):
    fetches = [
        pltpu.make_async_copy(source, target, arrived.at[n])
        for n, (source, target) in enumerate(
            (
                (profile_in, profile),
                (table_in, table),
                (k_in, k),
                (v_in, v),
                (q_in, q),
                (g_in, g),
            )
        )
    ]
    for fetch in fetches:
        fetch.start()
    fetches[0].wait()
    fetches[1].wait()
    w = level_weights(table, profile[...], width)
    w_out[...] = w
    fetches[2].wait()
    fetches[3].wait()
    for h in range(heads):
        lanes = slice(h * width, (h + 1) * width)
        ends_out[0, h] = contract(k[:, lanes], v[:, lanes], 0, 0)
    fetches[4].wait()
    fetches[5].wait()
    for h in range(heads):
        lanes = slice(h * width, (h + 1) * width)
        ends_out[1, h] = contract(g[:, lanes], weighted(q[:, lanes], w, h, top), 0, 0)


def second_kernel(first_far, width, heads, far, w, q, g, low_out, middle_out):
    for h in range(heads):
        lanes = slice(h * width, (h + 1) * width)
        stack = [weighted(q[:, lanes], w, h, first_far + j) for j in range(far - 1)]
        states = contract(g[:, lanes], jnp.concatenate(stack, axis=1), 0, 0)
        low_out[h] = states[:, :width]
        for j in range(1, far - 1):
            middle_out[j - 1, h] = states[:, j * width : (j + 1) * width]


def block_mask(w, levels, causal):
    parts = []
    for i in range(BLOCK // SMALL):
        rows = w[i * SMALL : (i + 1) * SMALL]
        tri = jnp.broadcast_to(rows[:, 0:1], (SMALL, SMALL))
        for l in range(1, SMALL.bit_length()):
            tri = jnp.where(levels >= l, rows[:, l : l + 1], tri)
        line = []
        for j in range(BLOCK // SMALL):
            if j > i:
                line.append(jnp.zeros((SMALL, SMALL), F32))
            elif j == i:
                line.append(jnp.where(causal, tri, 0.0))
            else:
                l = SMALL.bit_length() - 1 + (i ^ j).bit_length()
                line.append(jnp.broadcast_to(rows[:, l : l + 1], (SMALL, SMALL)))
        parts.append(jnp.concatenate(line, axis=1))
    return jnp.concatenate(parts, axis=0)


def merge_kernel(count, place, own_part, from_other, *sums):
    own = place[0]
    for l in range(count):
        taken = ((own & 1) == 1) & ((own >> l + 1 & 1) == 1)
        sums[l][...] = jnp.where(taken, own_part[l] + from_other[l], 0.0)


def tile_kernel(i, width, heads, depth, first_far, place, w, q, k, v, g, ends, out, dq, dk, dv):
    tokens = q.shape[0]
    on_first = (place[0] & 1) == 0
    places_t = lax.broadcasted_iota(jnp.int32, (SMALL, SMALL), 0)
    places_s = lax.broadcasted_iota(jnp.int32, (SMALL, SMALL), 1)
    differ = places_t ^ places_s
    levels = jnp.zeros((SMALL, SMALL), jnp.int32)
    for p in range(SMALL.bit_length() - 1):
        levels = levels + jnp.where(differ >= 1 << p, 1, 0)
    causal = places_s <= places_t
    rows = slice(i * BLOCK, (i + 1) * BLOCK)
    for h in range(heads):
        lanes = slice(h * width, (h + 1) * width)
        first = h * STRIDE
        qb, kb, vb, gb = q[rows, lanes], k[rows, lanes], v[rows, lanes], g[rows, lanes]
        mask = block_mask(w[rows, first : first + depth], levels, causal)
        probs = (contract(qb, kb, 1, 1) * mask).astype(BF16)
        grads = (contract(gb, vb, 1, 1) * mask).astype(BF16)
        state = jnp.where(on_first, 0.0, ends[0, h]).astype(BF16)
        scale = w[rows, first + first_far : first + first_far + 1]
        o = contract(probs, vb, 1, 0) + scale * contract(qb, state, 1, 0)
        d = contract(grads, kb, 1, 0) + scale * contract(gb, state, 1, 1)
        s = contract(grads, qb, 0, 0)
        e = contract(probs, gb, 0, 0)
        size = BLOCK
        while size < tokens:
            group = i * BLOCK // size
            sibling = slice((group ^ 1) * size, ((group ^ 1) + 1) * size)
            at = first + size.bit_length()
            if group & 1:
                scale = w[rows, at : at + 1]
                state = contract(k[sibling, lanes], v[sibling, lanes], 0, 0).astype(BF16)
                o = o + scale * contract(qb, state, 1, 0)
                d = d + scale * contract(gb, state, 1, 1)
            else:
                scaled = (q[sibling, lanes].astype(F32) * w[sibling, at : at + 1]).astype(BF16)
                pulled = contract(g[sibling, lanes], scaled, 0, 0).astype(BF16)
                s = s + contract(vb, pulled, 1, 0)
                e = e + contract(kb, pulled, 1, 1)
            size *= 2
        out[:, lanes] = o
        dq[:, lanes] = d
        dk[:, lanes] = s
        dv[:, lanes] = e


def far_kernel(
    width, heads, count, first_far, place, w, q, g, stacked, handed, *refs
):
    own = place[0]
    on_first = (own & 1) == 0
    local, (out, dq, near, arrived) = refs[:-4], refs[-4:]
    fetches = [pltpu.make_async_copy(part, near.at[n], arrived.at[n]) for n, part in enumerate(local)]
    for fetch in fetches:
        fetch.start()
    states = []
    for h in range(heads):
        of_head = []
        for j in range(1, count + 1):
            state = jnp.where(on_first, stacked[j - 1, h], handed[j - 1, h])
            of_head.append(jnp.where((own >> j & 1) == 1, state, 0.0).astype(BF16))
        states.append((jnp.concatenate(of_head, axis=0), jnp.concatenate(of_head, axis=1)))
    for i in range(q.shape[0] // BLOCK):
        rows = slice(i * BLOCK, (i + 1) * BLOCK)
        fetches[2 * i].wait()
        fetches[2 * i + 1].wait()
        for h in range(heads):
            lanes = slice(h * width, (h + 1) * width)
            scaled_q = [weighted(q[rows, lanes], w[rows, :], h, first_far + j) for j in range(1, count + 1)]
            scaled_g = [weighted(g[rows, lanes], w[rows, :], h, first_far + j) for j in range(1, count + 1)]
            tall, broad = states[h]
            o = contract(jnp.concatenate(scaled_q, axis=1), tall, 1, 0)
            d = contract(jnp.concatenate(scaled_g, axis=1), broad, 1, 1)
            out[rows, lanes] = near[2 * i, :, lanes] + o
            dq[rows, lanes] = near[2 * i + 1, :, lanes] + d


def more_kernel(width, heads, level, first_far, place, w, q, g, here, there, f_out, f_dq, out, dq):
    own = place[0]
    on_first = (own & 1) == 0
    for h in range(heads):
        lanes = slice(h * width, (h + 1) * width)
        state = jnp.where(on_first, here[h], there[h])
        state = jnp.where((own >> level & 1) == 1, state, 0.0).astype(BF16)
        scaled_q = weighted(q[:, lanes], w, h, first_far + level)
        scaled_g = weighted(g[:, lanes], w, h, first_far + level)
        out[:, lanes] = f_out[:, lanes] + contract(scaled_q, state, 1, 0)
        dq[:, lanes] = f_dq[:, lanes] + contract(scaled_g, state, 1, 1)


def last_kernel(
    width, heads, far, first_far, place, w, q, k, v, g, alone, top, alone_in, final, carried,
    far_out, far_dq, *refs,
):
    own = place[0]
    on_first = (own & 1) == 0
    local, (out, dq, dk, dv, near, arrived) = refs[:-6], refs[-6:]
    step = pl.program_id(0)
    fetches = [pltpu.make_async_copy(part, near.at[n], arrived.at[n]) for n, part in enumerate(local)]

    @pl.when(step == 0)
    def _():
        for fetch in fetches:
            fetch.start()

    for i in range(q.shape[0] // BLOCK):

        @pl.when(step == i)
        def _(i=i):
            rows = slice(i * BLOCK, (i + 1) * BLOCK)
            sums = []
            for h in range(heads):
                lanes = slice(h * width, (h + 1) * width)
                pair = []
                for j, here, there in ((far - 2, alone, alone_in), (far - 1, top, final)):
                    state = jnp.where(on_first, here[h], there[h])
                    pair.append(jnp.where((own >> j & 1) == 1, state, 0.0).astype(BF16))
                pulled = jnp.where(on_first, final[h], carried[h]).astype(BF16)
                scaled_q = [weighted(q[rows, lanes], w[rows, :], h, first_far + j) for j in (far - 2, far - 1)]
                scaled_g = [weighted(g[rows, lanes], w[rows, :], h, first_far + j) for j in (far - 2, far - 1)]
                o = contract(jnp.concatenate(scaled_q, axis=1), jnp.concatenate(pair, axis=0), 1, 0)
                d = contract(jnp.concatenate(scaled_g, axis=1), jnp.concatenate(pair, axis=1), 1, 1)
                out[:, lanes] = far_out[rows, lanes] + o
                dq[:, lanes] = far_dq[rows, lanes] + d
                sums.append((contract(v[rows, lanes], pulled, 1, 0), contract(k[rows, lanes], pulled, 1, 1)))
            fetches[2 * i].wait()
            fetches[2 * i + 1].wait()
            for h in range(heads):
                lanes = slice(h * width, (h + 1) * width)
                dk[:, lanes] = near[2 * i, :, lanes] + sums[h][0]
                dv[:, lanes] = near[2 * i + 1, :, lanes] + sums[h][1]


def links(row_bits, col_bits):
    steps = []
    place = 1
    while place < row_bits:
        steps.append(1 << place)
        if place + 1 < row_bits:
            steps.append(3 << place)
        place += 2
    for bit in range(col_bits):
        if bit == col_bits - 1 and bit > 0:
            steps.append(3 << row_bits + bit - 1)
        else:
            steps.append(1 << row_bits + bit)
    return steps


def tie(*trees):
    return lax.optimization_barrier(trees)


def shards(row_size, col_size, queries, keys, values, out_grad, weight_table, profile):
    tokens, columns = queries.shape
    _, heads, depth = weight_table.shape
    width = columns // heads
    row_bits = row_size.bit_length() - 1
    col_bits = col_size.bit_length() - 1
    far = row_bits + col_bits
    first_far = tokens.bit_length()
    devices = row_size * col_size
    own = lax.axis_index("col") * row_size + lax.axis_index("row")
    core = own & 1
    on_first = core == 0
    profile_row = profile.reshape(1, tokens)
    table = jnp.transpose(weight_table, (2, 1, 0))

    def full(shape, kind=F32):
        return jax.ShapeDtypeStruct(shape, kind)

    square = (heads, width, width)
    unit = tokens * width * width * heads * 2
    array = tokens * columns * 2
    exchange = [(i, i ^ 1) for i in range(devices)]

    weights, ends = call(
        functools.partial(first_kernel, first_far + far - 1, width, heads),
        (full((tokens, heads * STRIDE)), full((2,) + square)),
        3 * unit,
        4 * array,
        in_specs=[HBM] * 6,
        out_specs=[VMEM] * 2,
        scratch_shapes=[
            pltpu.VMEM(profile_row.shape, jnp.int32),
            pltpu.VMEM(table.shape, F32),
        ]
        + [pltpu.VMEM((tokens, columns), BF16)] * 4
        + [pltpu.SemaphoreType.DMA((6,))],
    )(*outside(profile_row, table, queries, keys, values, out_grad))
    other = lax.ppermute(ends, AXES, exchange)

    def second(w, q, g):
        return call(
            functools.partial(second_kernel, first_far, width, heads, far),
            (full(square), full((far - 2,) + square)),
            far * unit,
            4 * array,
            in_specs=[VMEM] * 3,
        )(w, q, g)

    smem = pl.BlockSpec(memory_space=pltpu.SMEM)
    place = own.reshape(1).astype(jnp.int32)
    blocks = tokens // BLOCK

    def tile(i, *operands):
        return call(
            functools.partial(tile_kernel, i, width, heads, depth, first_far),
            [full((BLOCK, columns))] * 4,
            20 * BLOCK * BLOCK * columns,
            6 * array,
            in_specs=[smem] + [VMEM] * 5 + [pl.BlockSpec()],
        )(place, *operands)

    low_grads, middle = second(weights, queries, out_grad)
    other_middle = lax.ppermute(middle, AXES, exchange)

    def merge(own_part, from_other):
        return call(
            functools.partial(merge_kernel, far - 2),
            [full(square)] * (far - 2),
            far * width * width,
            array,
            in_specs=[smem] + [pl.BlockSpec()] * 2,
            out_specs=[VMEM] * (far - 2),
        )(place, own_part, from_other)

    steps = links(row_bits, col_bits)
    rounds = len(steps)
    carried = jnp.where(on_first, ends[0] + other[0], 0.0)
    received = []
    local = []
    for r in range(1, rounds + 1):
        if r == 1:
            is_upper = (core == 1) & ((own >> far - 1 & 1) == 1)
            send = carried + jnp.where(is_upper, ends[1] + other[1], 0.0)
            carried, send = tie(carried, send)
        else:
            send = carried + sums[far - r - 1]
        pairs = [
            (i, i ^ (steps[rounds - r] if i & 1 else steps[r - 1])) for i in range(devices)
        ]
        if r > 1:
            (send,) = tie(send)
        got = lax.ppermute(send, AXES, pairs)
        after = (got,)
        if r == 1:
            sums = merge(middle, other_middle)
            after += (sums,)
        if r <= blocks:
            part = tile(r - 1, *tie((weights, queries, keys, values, out_grad, other), send)[0])
            local += list(part)
            after += (part,)
        elif r == rounds - 2:
            stacked = jnp.stack(received)
            handed = lax.ppermute(stacked, AXES, exchange)
            after += (stacked, handed)
        elif r == rounds - 1:
            fifth = received[-1]
            fifth_in = lax.ppermute(fifth, AXES, exchange)
            firsts = outside(*[part for i in range(blocks) for part in local[4 * i : 4 * i + 2]])
            far_sums = call(
                functools.partial(far_kernel, width, heads, far - 4, first_far),
                [full((tokens, columns))] * 2,
                2 * (far - 4) * unit,
                8 * array,
                in_specs=[smem] + [VMEM] * 3 + [pl.BlockSpec()] * 2 + [HBM] * len(firsts),
                out_specs=[VMEM] * 2,
                scratch_shapes=[
                    pltpu.VMEM((len(firsts), BLOCK, columns), F32),
                    pltpu.SemaphoreType.DMA((len(firsts),)),
                ],
            )(place, weights, queries, out_grad, stacked, handed, *firsts)
            after += (fifth_in, far_sums)
        else:
            alone = received[-1]
            alone_in = lax.ppermute(alone, AXES, exchange)
            far_out, far_dq = call(
                functools.partial(more_kernel, width, heads, far - 3, first_far),
                [full((tokens, columns))] * 2,
                2 * unit,
                8 * array,
                in_specs=[smem] + [VMEM] * 7,
                out_specs=[VMEM] * 2,
            )(place, weights, queries, out_grad, fifth, fifth_in, *far_sums)
            after += (alone_in, far_out, far_dq)
        after = tie(*after)
        got = after[0]
        if r == 1:
            sums = after[1]
        if r == rounds - 1:
            far_sums = after[2]
        if r == rounds:
            far_out, far_dq = after[2:]
        received.append(got)
        carried = carried + got

    top = received[-1]
    final = lax.ppermute(jnp.where(on_first, top, carried + low_grads), AXES, exchange)

    wide = pl.BlockSpec((BLOCK, columns), lambda i: (i, 0))
    seconds = outside(*[part for i in range(blocks) for part in local[4 * i + 2 : 4 * i + 4]])
    return call(
        functools.partial(last_kernel, width, heads, far, first_far),
        [full((tokens, columns))] * 4,
        6 * unit,
        16 * array,
        grid=(blocks,),
        in_specs=[smem] + [VMEM] * 5 + [pl.BlockSpec()] * 5 + [VMEM] * 2 + [HBM] * len(seconds),
        out_specs=[wide] * 4,
        scratch_shapes=[
            pltpu.VMEM((len(seconds), BLOCK, columns), F32),
            pltpu.SemaphoreType.DMA((len(seconds),)),
        ],
    )(
        place, weights, queries, keys, values, out_grad, alone, top, alone_in, final, carried,
        far_out, far_dq, *seconds,
    )


def solution(mesh):
    spread = P(AXES, None)

    def body(*args):
        return shards(mesh.shape["row"], mesh.shape["col"], *args)

    return jax.shard_map(
        body,
        mesh=mesh,
        in_specs=(spread,) * 4 + (P(), P(AXES)),
        out_specs=(spread,) * 4,
        check_vma=False,
    )
```

```python
import functools
import math

import jax
import jax.numpy as jnp
from jax import lax
from jax.experimental import pallas as pl
from jax.experimental.pallas import tpu as pltpu
from jax.sharding import PartitionSpec as P


F32 = jnp.float32
BF16 = jnp.bfloat16
AXES = ("col", "row")
BLOCK = 256
SMALL = 128
STRIDE = 64
ROOM = 16 << 20
VMEM = pl.BlockSpec(memory_space=pltpu.VMEM)
HBM = pl.BlockSpec(memory_space=pltpu.HBM)


def contract(a, b, dim_a, dim_b):
    return lax.dot_general(
        a, b, (((dim_a,), (dim_b,)), ((), ())), preferred_element_type=F32
    )


def outside(*arrays):
    return [pltpu.with_memory_space_constraint(x, pltpu.HBM) for x in arrays]


def call(kernel, out_shape, flops, moved, **rest):
    return pl.pallas_call(
        kernel,
        out_shape=out_shape,
        cost_estimate=pl.CostEstimate(flops=flops, bytes_accessed=moved, transcendentals=0),
        compiler_params=pltpu.CompilerParams(vmem_limit_bytes=ROOM),
        **rest,
    )


def level_weights(table, profile_row, width):
    levels, heads, profiles = table.shape
    places = lax.broadcasted_iota(jnp.int32, (profiles, profile_row.shape[1]), 0)
    onehot = jnp.where(places == profile_row, 1.0, 0.0).astype(BF16)
    blank = jnp.zeros((STRIDE - levels, profiles), F32)
    rows = []
    for h in range(heads):
        rows += [table[:, h, :], blank]
    rows = jnp.concatenate(rows, axis=0)
    high = rows.astype(BF16)
    rest = rows - high.astype(F32)
    middle = rest.astype(BF16)
    low = (rest - middle.astype(F32)).astype(BF16)
    picked = (contract(onehot, high, 0, 1) + contract(onehot, middle, 0, 1)) + contract(
        onehot, low, 0, 1
    )
    depth = (lax.broadcasted_iota(jnp.int32, (1, heads * STRIDE), 1) & (STRIDE - 1)).astype(F32)
    return picked * (jnp.exp2(-0.5 * depth) / math.sqrt(width))


def weighted(x, w, h, level):
    at = h * STRIDE + level
    return (x.astype(F32) * w[:, at : at + 1]).astype(BF16)


def first_kernel(
    top, width, heads, profile_in, table_in, q_in, k_in, v_in, g_in, w_out, ends_out,
    profile, table, q, k, v, g, arrived,
):
    fetches = [
        pltpu.make_async_copy(source, target, arrived.at[n])
        for n, (source, target) in enumerate(
            (
                (profile_in, profile),
                (table_in, table),
                (k_in, k),
                (v_in, v),
                (q_in, q),
                (g_in, g),
            )
        )
    ]
    for fetch in fetches:
        fetch.start()
    fetches[0].wait()
    fetches[1].wait()
    w = level_weights(table, profile[...], width)
    w_out[...] = w
    fetches[2].wait()
    fetches[3].wait()
    for h in range(heads):
        lanes = slice(h * width, (h + 1) * width)
        ends_out[0, h] = contract(k[:, lanes], v[:, lanes], 0, 0)
    fetches[4].wait()
    fetches[5].wait()
    for h in range(heads):
        lanes = slice(h * width, (h + 1) * width)
        ends_out[1, h] = contract(g[:, lanes], weighted(q[:, lanes], w, h, top), 0, 0)


def second_kernel(first_far, width, heads, far, w, q, g, low_out, middle_out):
    for h in range(heads):
        lanes = slice(h * width, (h + 1) * width)
        stack = [weighted(q[:, lanes], w, h, first_far + j) for j in range(far - 1)]
        states = contract(g[:, lanes], jnp.concatenate(stack, axis=1), 0, 0)
        low_out[h] = states[:, :width]
        for j in range(1, far - 1):
            middle_out[j - 1, h] = states[:, j * width : (j + 1) * width]


def block_mask(w, levels, causal):
    parts = []
    for i in range(BLOCK // SMALL):
        rows = w[i * SMALL : (i + 1) * SMALL]
        tri = jnp.broadcast_to(rows[:, 0:1], (SMALL, SMALL))
        for l in range(1, SMALL.bit_length()):
            tri = jnp.where(levels >= l, rows[:, l : l + 1], tri)
        line = []
        for j in range(BLOCK // SMALL):
            if j > i:
                line.append(jnp.zeros((SMALL, SMALL), F32))
            elif j == i:
                line.append(jnp.where(causal, tri, 0.0))
            else:
                l = SMALL.bit_length() - 1 + (i ^ j).bit_length()
                line.append(jnp.broadcast_to(rows[:, l : l + 1], (SMALL, SMALL)))
        parts.append(jnp.concatenate(line, axis=1))
    return jnp.concatenate(parts, axis=0)


def merge_kernel(count, place, own_part, from_other, *sums):
    own = place[0]
    for l in range(count):
        taken = ((own & 1) == 1) & ((own >> l + 1 & 1) == 1)
        sums[l][...] = jnp.where(taken, own_part[l] + from_other[l], 0.0)


def tile_kernel(i, width, heads, depth, first_far, place, w, q, k, v, g, ends, out, dq, dk, dv):
    tokens = q.shape[0]
    on_first = (place[0] & 1) == 0
    places_t = lax.broadcasted_iota(jnp.int32, (SMALL, SMALL), 0)
    places_s = lax.broadcasted_iota(jnp.int32, (SMALL, SMALL), 1)
    differ = places_t ^ places_s
    levels = jnp.zeros((SMALL, SMALL), jnp.int32)
    for p in range(SMALL.bit_length() - 1):
        levels = levels + jnp.where(differ >= 1 << p, 1, 0)
    causal = places_s <= places_t
    rows = slice(i * BLOCK, (i + 1) * BLOCK)
    for h in range(heads):
        lanes = slice(h * width, (h + 1) * width)
        first = h * STRIDE
        qb, kb, vb, gb = q[rows, lanes], k[rows, lanes], v[rows, lanes], g[rows, lanes]
        mask = block_mask(w[rows, first : first + depth], levels, causal)
        probs = (contract(qb, kb, 1, 1) * mask).astype(BF16)
        grads = (contract(gb, vb, 1, 1) * mask).astype(BF16)
        state = jnp.where(on_first, 0.0, ends[0, h]).astype(BF16)
        scale = w[rows, first + first_far : first + first_far + 1]
        o = contract(probs, vb, 1, 0) + scale * contract(qb, state, 1, 0)
        d = contract(grads, kb, 1, 0) + scale * contract(gb, state, 1, 1)
        s = contract(grads, qb, 0, 0)
        e = contract(probs, gb, 0, 0)
        size = BLOCK
        while size < tokens:
            group = i * BLOCK // size
            sibling = slice((group ^ 1) * size, ((group ^ 1) + 1) * size)
            at = first + size.bit_length()
            if group & 1:
                scale = w[rows, at : at + 1]
                state = contract(k[sibling, lanes], v[sibling, lanes], 0, 0).astype(BF16)
                o = o + scale * contract(qb, state, 1, 0)
                d = d + scale * contract(gb, state, 1, 1)
            else:
                scaled = (q[sibling, lanes].astype(F32) * w[sibling, at : at + 1]).astype(BF16)
                pulled = contract(g[sibling, lanes], scaled, 0, 0).astype(BF16)
                s = s + contract(vb, pulled, 1, 0)
                e = e + contract(kb, pulled, 1, 1)
            size *= 2
        out[:, lanes] = o
        dq[:, lanes] = d
        dk[:, lanes] = s
        dv[:, lanes] = e


def far_kernel(width, heads, count, first_far, axis, place, w, x, stacked, handed, *refs):
    own = place[0]
    on_first = (own & 1) == 0
    local, (total, near, arrived) = refs[:-3], refs[-3:]
    fetches = [pltpu.make_async_copy(part, near.at[n], arrived.at[n]) for n, part in enumerate(local)]
    for fetch in fetches:
        fetch.start()
    states = []
    for h in range(heads):
        of_head = []
        for j in range(1, count + 1):
            state = jnp.where(on_first, stacked[j - 1, h], handed[j - 1, h])
            of_head.append(jnp.where((own >> j & 1) == 1, state, 0.0).astype(BF16))
        states.append(jnp.concatenate(of_head, axis=axis))
    for i in range(x.shape[0] // BLOCK):
        rows = slice(i * BLOCK, (i + 1) * BLOCK)
        fetches[i].wait()
        for h in range(heads):
            lanes = slice(h * width, (h + 1) * width)
            scaled = [weighted(x[rows, lanes], w[rows, :], h, first_far + j) for j in range(1, count + 1)]
            total[rows, lanes] = near[i, :, lanes] + contract(
                jnp.concatenate(scaled, axis=1), states[h], 1, axis
            )


def more_kernel(width, heads, first, first_far, place, w, q, g, fifth, fifth_in, alone, alone_in, f_out, f_dq, out, dq):
    own = place[0]
    on_first = (own & 1) == 0
    for h in range(heads):
        lanes = slice(h * width, (h + 1) * width)
        pair, scaled_q, scaled_g = [], [], []
        for j, here, there in ((first, fifth, fifth_in), (first + 1, alone, alone_in)):
            state = jnp.where(on_first, here[h], there[h])
            pair.append(jnp.where((own >> j & 1) == 1, state, 0.0).astype(BF16))
            scaled_q.append(weighted(q[:, lanes], w, h, first_far + j))
            scaled_g.append(weighted(g[:, lanes], w, h, first_far + j))
        o = contract(jnp.concatenate(scaled_q, axis=1), jnp.concatenate(pair, axis=0), 1, 0)
        d = contract(jnp.concatenate(scaled_g, axis=1), jnp.concatenate(pair, axis=1), 1, 1)
        out[:, lanes] = f_out[:, lanes] + o
        dq[:, lanes] = f_dq[:, lanes] + d


def last_kernel(
    width, heads, far, first_far, place, w, q, k, v, g, top, final, carried, far_out, far_dq, *refs
):
    own = place[0]
    local, (out, dq, dk, dv, near, arrived, state, pulled) = refs[:-8], refs[-8:]
    step = pl.program_id(0)
    fetches = [pltpu.make_async_copy(part, near.at[n], arrived.at[n]) for n, part in enumerate(local)]

    @pl.when(step == 0)
    def _():
        for fetch in fetches:
            fetch.start()
        on_first = (own & 1) == 0
        for h in range(heads):
            highest = jnp.where(on_first, top[h], final[h])
            state[h] = jnp.where((own >> far - 1 & 1) == 1, highest, 0.0).astype(BF16)
            pulled[h] = jnp.where(on_first, final[h], carried[h]).astype(BF16)

    for i in range(q.shape[0] // BLOCK):

        @pl.when(step == i)
        def _(i=i):
            rows = slice(i * BLOCK, (i + 1) * BLOCK)
            fetches[2 * i].wait()
            fetches[2 * i + 1].wait()
            for h in range(heads):
                lanes = slice(h * width, (h + 1) * width)
                at = h * STRIDE + first_far + far - 1
                scale = w[rows, at : at + 1]
                out[:, lanes] = far_out[rows, lanes] + scale * contract(q[rows, lanes], state[h], 1, 0)
                dq[:, lanes] = far_dq[rows, lanes] + scale * contract(g[rows, lanes], state[h], 1, 1)
                dk[:, lanes] = near[2 * i, :, lanes] + contract(v[rows, lanes], pulled[h], 1, 0)
                dv[:, lanes] = near[2 * i + 1, :, lanes] + contract(k[rows, lanes], pulled[h], 1, 1)


def links(row_bits, col_bits):
    steps = []
    place = 1
    while place < row_bits:
        steps.append(1 << place)
        if place + 1 < row_bits:
            steps.append(3 << place)
        place += 2
    for bit in range(col_bits):
        if bit == col_bits - 1 and bit > 0:
            steps.append(3 << row_bits + bit - 1)
        else:
            steps.append(1 << row_bits + bit)
    return steps


def tie(*trees):
    return lax.optimization_barrier(trees)


def shards(row_size, col_size, queries, keys, values, out_grad, weight_table, profile):
    tokens, columns = queries.shape
    _, heads, depth = weight_table.shape
    width = columns // heads
    row_bits = row_size.bit_length() - 1
    col_bits = col_size.bit_length() - 1
    far = row_bits + col_bits
    first_far = tokens.bit_length()
    devices = row_size * col_size
    own = lax.axis_index("col") * row_size + lax.axis_index("row")
    core = own & 1
    on_first = core == 0
    profile_row = profile.reshape(1, tokens)
    table = jnp.transpose(weight_table, (2, 1, 0))

    def full(shape, kind=F32):
        return jax.ShapeDtypeStruct(shape, kind)

    square = (heads, width, width)
    unit = tokens * width * width * heads * 2
    array = tokens * columns * 2
    exchange = [(i, i ^ 1) for i in range(devices)]

    weights, ends = call(
        functools.partial(first_kernel, first_far + far - 1, width, heads),
        (full((tokens, heads * STRIDE)), full((2,) + square)),
        3 * unit,
        4 * array,
        in_specs=[HBM] * 6,
        out_specs=[VMEM] * 2,
        scratch_shapes=[
            pltpu.VMEM(profile_row.shape, jnp.int32),
            pltpu.VMEM(table.shape, F32),
        ]
        + [pltpu.VMEM((tokens, columns), BF16)] * 4
        + [pltpu.SemaphoreType.DMA((6,))],
    )(*outside(profile_row, table, queries, keys, values, out_grad))
    other = lax.ppermute(ends, AXES, exchange)

    def second(w, q, g):
        return call(
            functools.partial(second_kernel, first_far, width, heads, far),
            (full(square), full((far - 2,) + square)),
            far * unit,
            4 * array,
            in_specs=[VMEM] * 3,
        )(w, q, g)

    smem = pl.BlockSpec(memory_space=pltpu.SMEM)
    place = own.reshape(1).astype(jnp.int32)
    blocks = tokens // BLOCK

    def tile(i, *operands):
        return call(
            functools.partial(tile_kernel, i, width, heads, depth, first_far),
            [full((BLOCK, columns))] * 4,
            20 * BLOCK * BLOCK * columns,
            6 * array,
            in_specs=[smem] + [VMEM] * 5 + [pl.BlockSpec()],
        )(place, *operands)

    low_grads, middle = second(weights, queries, out_grad)
    other_middle = lax.ppermute(middle, AXES, exchange)

    def merge(own_part, from_other):
        return call(
            functools.partial(merge_kernel, far - 2),
            [full(square)] * (far - 2),
            far * width * width,
            array,
            in_specs=[smem] + [pl.BlockSpec()] * 2,
            out_specs=[VMEM] * (far - 2),
        )(place, own_part, from_other)

    def add_far(axis, x, stacked, handed):
        parts = outside(*[local[4 * i + axis] for i in range(blocks)])
        return call(
            functools.partial(far_kernel, width, heads, far - 4, first_far, axis),
            full((tokens, columns)),
            (far - 4) * unit,
            4 * array,
            in_specs=[smem] + [VMEM] * 2 + [pl.BlockSpec()] * 2 + [HBM] * blocks,
            out_specs=VMEM,
            scratch_shapes=[
                pltpu.VMEM((blocks, BLOCK, columns), F32),
                pltpu.SemaphoreType.DMA((blocks,)),
            ],
        )(place, weights, x, stacked, handed, *parts)

    steps = links(row_bits, col_bits)
    rounds = len(steps)
    carried = jnp.where(on_first, ends[0] + other[0], 0.0)
    received = []
    local = []
    for r in range(1, rounds + 1):
        if r == 1:
            is_upper = (core == 1) & ((own >> far - 1 & 1) == 1)
            send = carried + jnp.where(is_upper, ends[1] + other[1], 0.0)
            carried, send = tie(carried, send)
        else:
            send = carried + sums[far - r - 1]
        pairs = [
            (i, i ^ (steps[rounds - r] if i & 1 else steps[r - 1])) for i in range(devices)
        ]
        if r > 1:
            (send,) = tie(send)
        got = lax.ppermute(send, AXES, pairs)
        after = (got,)
        if r == 1:
            sums = merge(middle, other_middle)
            after += (sums,)
        if r <= blocks:
            part = tile(r - 1, *tie((weights, queries, keys, values, out_grad, other), send)[0])
            local += list(part)
            after += (part,)
        elif r == rounds - 2:
            stacked = jnp.stack(received)
            handed = lax.ppermute(stacked, AXES, exchange)
            after += (stacked, handed)
        elif r == rounds - 1:
            fifth = received[-1]
            fifth_in = lax.ppermute(fifth, AXES, exchange)
            far_out = add_far(0, queries, stacked, handed)
            after += (fifth_in, far_out)
        else:
            alone = received[-1]
            alone_in = lax.ppermute(alone, AXES, exchange)
            far_dq = add_far(1, out_grad, stacked, handed)
            far_out, far_dq = call(
                functools.partial(more_kernel, width, heads, far - 3, first_far),
                [full((tokens, columns))] * 2,
                4 * unit,
                8 * array,
                in_specs=[smem] + [VMEM] * 9,
                out_specs=[VMEM] * 2,
            )(
                place, weights, queries, out_grad, fifth, fifth_in, alone, alone_in,
                far_out, far_dq,
            )
            after += (alone_in, far_out, far_dq)
        after = tie(*after)
        got = after[0]
        if r == 1:
            sums = after[1]
        if r == rounds - 1:
            far_out = after[2]
        if r == rounds:
            far_out, far_dq = after[2:]
        received.append(got)
        carried = carried + got

    top = received[-1]
    final = lax.ppermute(jnp.where(on_first, top, carried + low_grads), AXES, exchange)

    wide = pl.BlockSpec((BLOCK, columns), lambda i: (i, 0))
    seconds = outside(*[part for i in range(blocks) for part in local[4 * i + 2 : 4 * i + 4]])
    return call(
        functools.partial(last_kernel, width, heads, far, first_far),
        [full((tokens, columns))] * 4,
        6 * unit,
        16 * array,
        grid=(blocks,),
        in_specs=[smem] + [VMEM] * 5 + [pl.BlockSpec()] * 3 + [VMEM] * 2 + [HBM] * len(seconds),
        out_specs=[wide] * 4,
        scratch_shapes=[
            pltpu.VMEM((len(seconds), BLOCK, columns), F32),
            pltpu.SemaphoreType.DMA((len(seconds),)),
            pltpu.VMEM(square, BF16),
            pltpu.VMEM(square, BF16),
        ],
    )(
        place, weights, queries, keys, values, out_grad, top, final, carried,
        far_out, far_dq, *seconds,
    )


def solution(mesh):
    spread = P(AXES, None)

    def body(*args):
        return shards(mesh.shape["row"], mesh.shape["col"], *args)

    return jax.shard_map(
        body,
        mesh=mesh,
        in_specs=(spread,) * 4 + (P(), P(AXES)),
        out_specs=(spread,) * 4,
        check_vma=False,
    )
```

```python
import functools
import math

import jax
import jax.numpy as jnp
from jax import lax
from jax.experimental import pallas as pl
from jax.experimental.pallas import tpu as pltpu
from jax.sharding import PartitionSpec as P


F32 = jnp.float32
BF16 = jnp.bfloat16
AXES = ("col", "row")
BLOCK = 256
SMALL = 128
STRIDE = 64
ROOM = 16 << 20
VMEM = pl.BlockSpec(memory_space=pltpu.VMEM)
HBM = pl.BlockSpec(memory_space=pltpu.HBM)


def contract(a, b, dim_a, dim_b):
    return lax.dot_general(
        a, b, (((dim_a,), (dim_b,)), ((), ())), preferred_element_type=F32
    )


def outside(*arrays):
    return [pltpu.with_memory_space_constraint(x, pltpu.HBM) for x in arrays]


def call(kernel, out_shape, flops, moved, **rest):
    return pl.pallas_call(
        kernel,
        out_shape=out_shape,
        cost_estimate=pl.CostEstimate(flops=flops, bytes_accessed=moved, transcendentals=0),
        compiler_params=pltpu.CompilerParams(vmem_limit_bytes=ROOM),
        **rest,
    )


def level_weights(table, profile_row, width):
    levels, heads, profiles = table.shape
    places = lax.broadcasted_iota(jnp.int32, (profiles, profile_row.shape[1]), 0)
    onehot = jnp.where(places == profile_row, 1.0, 0.0).astype(BF16)
    blank = jnp.zeros((STRIDE - levels, profiles), F32)
    rows = []
    for h in range(heads):
        rows += [table[:, h, :], blank]
    rows = jnp.concatenate(rows, axis=0)
    high = rows.astype(BF16)
    rest = rows - high.astype(F32)
    middle = rest.astype(BF16)
    low = (rest - middle.astype(F32)).astype(BF16)
    picked = (contract(onehot, high, 0, 1) + contract(onehot, middle, 0, 1)) + contract(
        onehot, low, 0, 1
    )
    depth = (lax.broadcasted_iota(jnp.int32, (1, heads * STRIDE), 1) & (STRIDE - 1)).astype(F32)
    return picked * (jnp.exp2(-0.5 * depth) / math.sqrt(width))


def weighted(x, w, h, level):
    at = h * STRIDE + level
    return (x.astype(F32) * w[:, at : at + 1]).astype(BF16)


def first_kernel(
    top, width, heads, profile_in, table_in, q_in, k_in, v_in, g_in, w_out, ends_out,
    profile, table, q, k, v, g, arrived,
):
    fetches = [
        pltpu.make_async_copy(source, target, arrived.at[n])
        for n, (source, target) in enumerate(
            (
                (profile_in, profile),
                (table_in, table),
                (k_in, k),
                (v_in, v),
                (q_in, q),
                (g_in, g),
            )
        )
    ]
    for fetch in fetches:
        fetch.start()
    fetches[0].wait()
    fetches[1].wait()
    w = level_weights(table, profile[...], width)
    w_out[...] = w
    fetches[2].wait()
    fetches[3].wait()
    for h in range(heads):
        lanes = slice(h * width, (h + 1) * width)
        ends_out[0, h] = contract(k[:, lanes], v[:, lanes], 0, 0)
    fetches[4].wait()
    fetches[5].wait()
    for h in range(heads):
        lanes = slice(h * width, (h + 1) * width)
        ends_out[1, h] = contract(g[:, lanes], weighted(q[:, lanes], w, h, top), 0, 0)


def second_kernel(first_far, width, heads, far, w, q, g, low_out, middle_out):
    for h in range(heads):
        lanes = slice(h * width, (h + 1) * width)
        stack = [weighted(q[:, lanes], w, h, first_far + j) for j in range(far - 1)]
        states = contract(g[:, lanes], jnp.concatenate(stack, axis=1), 0, 0)
        low_out[h] = states[:, :width]
        for j in range(1, far - 1):
            middle_out[j - 1, h] = states[:, j * width : (j + 1) * width]


def block_mask(w, levels, causal):
    parts = []
    for i in range(BLOCK // SMALL):
        rows = w[i * SMALL : (i + 1) * SMALL]
        tri = jnp.broadcast_to(rows[:, 0:1], (SMALL, SMALL))
        for l in range(1, SMALL.bit_length()):
            tri = jnp.where(levels >= l, rows[:, l : l + 1], tri)
        line = []
        for j in range(BLOCK // SMALL):
            if j > i:
                line.append(jnp.zeros((SMALL, SMALL), F32))
            elif j == i:
                line.append(jnp.where(causal, tri, 0.0))
            else:
                l = SMALL.bit_length() - 1 + (i ^ j).bit_length()
                line.append(jnp.broadcast_to(rows[:, l : l + 1], (SMALL, SMALL)))
        parts.append(jnp.concatenate(line, axis=1))
    return jnp.concatenate(parts, axis=0)


def merge_kernel(count, place, own_part, from_other, *sums):
    own = place[0]
    for l in range(count):
        taken = ((own & 1) == 1) & ((own >> l + 1 & 1) == 1)
        sums[l][...] = jnp.where(taken, own_part[l] + from_other[l], 0.0)


def tile_kernel(i, width, heads, depth, first_far, place, w, q, k, v, g, ends, out, dq, dk, dv):
    tokens = q.shape[0]
    on_first = (place[0] & 1) == 0
    places_t = lax.broadcasted_iota(jnp.int32, (SMALL, SMALL), 0)
    places_s = lax.broadcasted_iota(jnp.int32, (SMALL, SMALL), 1)
    differ = places_t ^ places_s
    levels = jnp.zeros((SMALL, SMALL), jnp.int32)
    for p in range(SMALL.bit_length() - 1):
        levels = levels + jnp.where(differ >= 1 << p, 1, 0)
    causal = places_s <= places_t
    rows = slice(i * BLOCK, (i + 1) * BLOCK)
    for h in range(heads):
        lanes = slice(h * width, (h + 1) * width)
        first = h * STRIDE
        qb, kb, vb, gb = q[rows, lanes], k[rows, lanes], v[rows, lanes], g[rows, lanes]
        mask = block_mask(w[rows, first : first + depth], levels, causal)
        probs = (contract(qb, kb, 1, 1) * mask).astype(BF16)
        grads = (contract(gb, vb, 1, 1) * mask).astype(BF16)
        state = jnp.where(on_first, 0.0, ends[0, h]).astype(BF16)
        scale = w[rows, first + first_far : first + first_far + 1]
        o = contract(probs, vb, 1, 0) + scale * contract(qb, state, 1, 0)
        d = contract(grads, kb, 1, 0) + scale * contract(gb, state, 1, 1)
        s = contract(grads, qb, 0, 0)
        e = contract(probs, gb, 0, 0)
        size = BLOCK
        while size < tokens:
            group = i * BLOCK // size
            sibling = slice((group ^ 1) * size, ((group ^ 1) + 1) * size)
            at = first + size.bit_length()
            if group & 1:
                scale = w[rows, at : at + 1]
                state = contract(k[sibling, lanes], v[sibling, lanes], 0, 0).astype(BF16)
                o = o + scale * contract(qb, state, 1, 0)
                d = d + scale * contract(gb, state, 1, 1)
            else:
                scaled = (q[sibling, lanes].astype(F32) * w[sibling, at : at + 1]).astype(BF16)
                pulled = contract(g[sibling, lanes], scaled, 0, 0).astype(BF16)
                s = s + contract(vb, pulled, 1, 0)
                e = e + contract(kb, pulled, 1, 1)
            size *= 2
        out[:, lanes] = o
        dq[:, lanes] = d
        dk[:, lanes] = s
        dv[:, lanes] = e


def far_kernel(
    width, heads, count, first_far, place, w, q, g, stacked, handed, *refs
):
    own = place[0]
    on_first = (own & 1) == 0
    local, (out, dq, near, arrived) = refs[:-4], refs[-4:]
    fetches = [pltpu.make_async_copy(part, near.at[n], arrived.at[n]) for n, part in enumerate(local)]
    for fetch in fetches:
        fetch.start()
    states = []
    for h in range(heads):
        of_head = []
        for j in range(1, count + 1):
            state = jnp.where(on_first, stacked[j - 1, h], handed[j - 1, h])
            of_head.append(jnp.where((own >> j & 1) == 1, state, 0.0).astype(BF16))
        states.append((jnp.concatenate(of_head, axis=0), jnp.concatenate(of_head, axis=1)))
    for i in range(q.shape[0] // BLOCK):
        rows = slice(i * BLOCK, (i + 1) * BLOCK)
        fetches[2 * i].wait()
        fetches[2 * i + 1].wait()
        for h in range(heads):
            lanes = slice(h * width, (h + 1) * width)
            scaled_q = [weighted(q[rows, lanes], w[rows, :], h, first_far + j) for j in range(1, count + 1)]
            scaled_g = [weighted(g[rows, lanes], w[rows, :], h, first_far + j) for j in range(1, count + 1)]
            tall, broad = states[h]
            o = contract(jnp.concatenate(scaled_q, axis=1), tall, 1, 0)
            d = contract(jnp.concatenate(scaled_g, axis=1), broad, 1, 1)
            out[rows, lanes] = near[2 * i, :, lanes] + o
            dq[rows, lanes] = near[2 * i + 1, :, lanes] + d


def more_kernel(width, heads, first, first_far, place, w, q, g, fifth, fifth_in, alone, alone_in, f_out, f_dq, out, dq):
    own = place[0]
    on_first = (own & 1) == 0
    for h in range(heads):
        lanes = slice(h * width, (h + 1) * width)
        pair, scaled_q, scaled_g = [], [], []
        for j, here, there in ((first, fifth, fifth_in), (first + 1, alone, alone_in)):
            state = jnp.where(on_first, here[h], there[h])
            pair.append(jnp.where((own >> j & 1) == 1, state, 0.0).astype(BF16))
            scaled_q.append(weighted(q[:, lanes], w, h, first_far + j))
            scaled_g.append(weighted(g[:, lanes], w, h, first_far + j))
        o = contract(jnp.concatenate(scaled_q, axis=1), jnp.concatenate(pair, axis=0), 1, 0)
        d = contract(jnp.concatenate(scaled_g, axis=1), jnp.concatenate(pair, axis=1), 1, 1)
        out[:, lanes] = f_out[:, lanes] + o
        dq[:, lanes] = f_dq[:, lanes] + d


def last_kernel(
    width, heads, far, first_far, place, w, q, k, v, g, top, final, carried, far_out, far_dq, *refs
):
    own = place[0]
    local, (out, dq, dk, dv, near, arrived, state, pulled) = refs[:-8], refs[-8:]
    step = pl.program_id(0)
    fetches = [pltpu.make_async_copy(part, near.at[n], arrived.at[n]) for n, part in enumerate(local)]

    @pl.when(step == 0)
    def _():
        for fetch in fetches:
            fetch.start()
        on_first = (own & 1) == 0
        for h in range(heads):
            highest = jnp.where(on_first, top[h], final[h])
            state[h] = jnp.where((own >> far - 1 & 1) == 1, highest, 0.0).astype(BF16)
            pulled[h] = jnp.where(on_first, final[h], carried[h]).astype(BF16)

    for i in range(q.shape[0] // BLOCK):

        @pl.when(step == i)
        def _(i=i):
            rows = slice(i * BLOCK, (i + 1) * BLOCK)
            fetches[2 * i].wait()
            fetches[2 * i + 1].wait()
            for h in range(heads):
                lanes = slice(h * width, (h + 1) * width)
                at = h * STRIDE + first_far + far - 1
                scale = w[rows, at : at + 1]
                out[:, lanes] = far_out[rows, lanes] + scale * contract(q[rows, lanes], state[h], 1, 0)
                dq[:, lanes] = far_dq[rows, lanes] + scale * contract(g[rows, lanes], state[h], 1, 1)
                dk[:, lanes] = near[2 * i, :, lanes] + contract(v[rows, lanes], pulled[h], 1, 0)
                dv[:, lanes] = near[2 * i + 1, :, lanes] + contract(k[rows, lanes], pulled[h], 1, 1)


def links(row_bits, col_bits):
    steps = []
    place = 1
    while place < row_bits:
        steps.append(1 << place)
        if place + 1 < row_bits:
            steps.append(3 << place)
        place += 2
    for bit in range(col_bits):
        if bit == col_bits - 1 and bit > 0:
            steps.append(3 << row_bits + bit - 1)
        else:
            steps.append(1 << row_bits + bit)
    return steps


def tie(*trees):
    return lax.optimization_barrier(trees)


def shards(row_size, col_size, queries, keys, values, out_grad, weight_table, profile):
    tokens, columns = queries.shape
    _, heads, depth = weight_table.shape
    width = columns // heads
    row_bits = row_size.bit_length() - 1
    col_bits = col_size.bit_length() - 1
    far = row_bits + col_bits
    first_far = tokens.bit_length()
    devices = row_size * col_size
    own = lax.axis_index("col") * row_size + lax.axis_index("row")
    core = own & 1
    on_first = core == 0
    profile_row = profile.reshape(1, tokens)
    table = jnp.transpose(weight_table, (2, 1, 0))

    def full(shape, kind=F32):
        return jax.ShapeDtypeStruct(shape, kind)

    square = (heads, width, width)
    unit = tokens * width * width * heads * 2
    array = tokens * columns * 2
    exchange = [(i, i ^ 1) for i in range(devices)]

    weights, ends = call(
        functools.partial(first_kernel, first_far + far - 1, width, heads),
        (full((tokens, heads * STRIDE)), full((2,) + square)),
        3 * unit,
        4 * array,
        in_specs=[HBM] * 6,
        out_specs=[VMEM] * 2,
        scratch_shapes=[
            pltpu.VMEM(profile_row.shape, jnp.int32),
            pltpu.VMEM(table.shape, F32),
        ]
        + [pltpu.VMEM((tokens, columns), BF16)] * 4
        + [pltpu.SemaphoreType.DMA((6,))],
    )(*outside(profile_row, table, queries, keys, values, out_grad))
    other = lax.ppermute(ends, AXES, exchange)

    def second(w, q, g):
        return call(
            functools.partial(second_kernel, first_far, width, heads, far),
            (full(square), full((far - 2,) + square)),
            far * unit,
            4 * array,
            in_specs=[VMEM] * 3,
        )(w, q, g)

    smem = pl.BlockSpec(memory_space=pltpu.SMEM)
    place = own.reshape(1).astype(jnp.int32)
    blocks = tokens // BLOCK

    def tile(i, *operands):
        return call(
            functools.partial(tile_kernel, i, width, heads, depth, first_far),
            [full((BLOCK, columns))] * 4,
            20 * BLOCK * BLOCK * columns,
            6 * array,
            in_specs=[smem] + [VMEM] * 5 + [pl.BlockSpec()],
        )(place, *operands)

    low_grads, middle = second(weights, queries, out_grad)
    other_middle = lax.ppermute(middle, AXES, exchange)

    def merge(own_part, from_other):
        return call(
            functools.partial(merge_kernel, far - 2),
            [full(square)] * (far - 2),
            far * width * width,
            array,
            in_specs=[smem] + [pl.BlockSpec()] * 2,
            out_specs=[VMEM] * (far - 2),
        )(place, own_part, from_other)

    def add_far(stacked, handed):
        parts = outside(*[part for i in range(blocks) for part in local[4 * i : 4 * i + 2]])
        return call(
            functools.partial(far_kernel, width, heads, far - 4, first_far),
            [full((tokens, columns))] * 2,
            2 * (far - 4) * unit,
            8 * array,
            in_specs=[smem] + [VMEM] * 3 + [pl.BlockSpec()] * 2 + [HBM] * len(parts),
            out_specs=[VMEM] * 2,
            scratch_shapes=[
                pltpu.VMEM((len(parts), BLOCK, columns), F32),
                pltpu.SemaphoreType.DMA((len(parts),)),
            ],
        )(place, weights, queries, out_grad, stacked, handed, *parts)

    steps = links(row_bits, col_bits)
    rounds = len(steps)
    carried = jnp.where(on_first, ends[0] + other[0], 0.0)
    received = []
    local = []
    for r in range(1, rounds + 1):
        if r == 1:
            is_upper = (core == 1) & ((own >> far - 1 & 1) == 1)
            send = carried + jnp.where(is_upper, ends[1] + other[1], 0.0)
            carried, send = tie(carried, send)
        else:
            send = carried + sums[far - r - 1]
        pairs = [
            (i, i ^ (steps[rounds - r] if i & 1 else steps[r - 1])) for i in range(devices)
        ]
        if r > 1:
            (send,) = tie(send)
        got = lax.ppermute(send, AXES, pairs)
        after = (got,)
        if r == 1:
            sums = merge(middle, other_middle)
            after += (sums,)
        if r <= blocks:
            part = tile(r - 1, *tie((weights, queries, keys, values, out_grad, other), send)[0])
            local += list(part)
            after += (part,)
        elif r == rounds - 2:
            stacked = jnp.stack(received)
            handed = lax.ppermute(stacked, AXES, exchange)
            after += (stacked, handed)
        elif r == rounds - 1:
            far_sums = add_far(stacked, handed)
            after += (far_sums,)
        else:
            fifth, alone = received[-2:]
            fifth_in = lax.ppermute(fifth, AXES, exchange)
            alone_in = lax.ppermute(alone, AXES, exchange)
            far_out, far_dq = call(
                functools.partial(more_kernel, width, heads, far - 3, first_far),
                [full((tokens, columns))] * 2,
                4 * unit,
                8 * array,
                in_specs=[smem] + [VMEM] * 9,
                out_specs=[VMEM] * 2,
            )(
                place, weights, queries, out_grad, fifth, fifth_in, alone, alone_in,
                *far_sums,
            )
            after += (far_out, far_dq)
        after = tie(*after)
        got = after[0]
        if r == 1:
            sums = after[1]
        if r == rounds - 1:
            far_sums = after[1]
        if r == rounds:
            far_out, far_dq = after[1:]
        received.append(got)
        carried = carried + got

    top = received[-1]
    final = lax.ppermute(jnp.where(on_first, top, carried + low_grads), AXES, exchange)

    wide = pl.BlockSpec((BLOCK, columns), lambda i: (i, 0))
    seconds = outside(*[part for i in range(blocks) for part in local[4 * i + 2 : 4 * i + 4]])
    return call(
        functools.partial(last_kernel, width, heads, far, first_far),
        [full((tokens, columns))] * 4,
        6 * unit,
        16 * array,
        grid=(blocks,),
        in_specs=[smem] + [VMEM] * 5 + [pl.BlockSpec()] * 3 + [VMEM] * 2 + [HBM] * len(seconds),
        out_specs=[wide] * 4,
        scratch_shapes=[
            pltpu.VMEM((len(seconds), BLOCK, columns), F32),
            pltpu.SemaphoreType.DMA((len(seconds),)),
            pltpu.VMEM(square, BF16),
            pltpu.VMEM(square, BF16),
        ],
    )(
        place, weights, queries, keys, values, out_grad, top, final, carried,
        far_out, far_dq, *seconds,
    )


def solution(mesh):
    spread = P(AXES, None)

    def body(*args):
        return shards(mesh.shape["row"], mesh.shape["col"], *args)

    return jax.shard_map(
        body,
        mesh=mesh,
        in_specs=(spread,) * 4 + (P(), P(AXES)),
        out_specs=(spread,) * 4,
        check_vma=False,
    )
```

```python
import functools
import math

import jax
import jax.numpy as jnp
from jax import lax
from jax.experimental import pallas as pl
from jax.experimental.pallas import tpu as pltpu
from jax.sharding import PartitionSpec as P


F32 = jnp.float32
BF16 = jnp.bfloat16
AXES = ("col", "row")
BLOCK = 256
SMALL = 128
STRIDE = 64
ROOM = 16 << 20
VMEM = pl.BlockSpec(memory_space=pltpu.VMEM)
HBM = pl.BlockSpec(memory_space=pltpu.HBM)


def contract(a, b, dim_a, dim_b):
    return lax.dot_general(
        a, b, (((dim_a,), (dim_b,)), ((), ())), preferred_element_type=F32
    )


def outside(*arrays):
    return [pltpu.with_memory_space_constraint(x, pltpu.HBM) for x in arrays]


def call(kernel, out_shape, flops, moved, **rest):
    return pl.pallas_call(
        kernel,
        out_shape=out_shape,
        cost_estimate=pl.CostEstimate(flops=flops, bytes_accessed=moved, transcendentals=0),
        compiler_params=pltpu.CompilerParams(vmem_limit_bytes=ROOM),
        **rest,
    )


def level_weights(table, profile_row, width):
    levels, heads, profiles = table.shape
    places = lax.broadcasted_iota(jnp.int32, (profiles, profile_row.shape[1]), 0)
    onehot = jnp.where(places == profile_row, 1.0, 0.0).astype(BF16)
    blank = jnp.zeros((STRIDE - levels, profiles), F32)
    rows = []
    for h in range(heads):
        rows += [table[:, h, :], blank]
    rows = jnp.concatenate(rows, axis=0)
    high = rows.astype(BF16)
    rest = rows - high.astype(F32)
    middle = rest.astype(BF16)
    low = (rest - middle.astype(F32)).astype(BF16)
    picked = (contract(onehot, high, 0, 1) + contract(onehot, middle, 0, 1)) + contract(
        onehot, low, 0, 1
    )
    depth = (lax.broadcasted_iota(jnp.int32, (1, heads * STRIDE), 1) & (STRIDE - 1)).astype(F32)
    return picked * (jnp.exp2(-0.5 * depth) / math.sqrt(width))


def weighted(x, w, h, level):
    at = h * STRIDE + level
    return (x.astype(F32) * w[:, at : at + 1]).astype(BF16)


def first_kernel(
    top, width, heads, profile_in, table_in, q_in, k_in, v_in, g_in, w_out, ends_out,
    profile, table, q, k, v, g, arrived,
):
    fetches = [
        pltpu.make_async_copy(source, target, arrived.at[n])
        for n, (source, target) in enumerate(
            (
                (profile_in, profile),
                (table_in, table),
                (k_in, k),
                (v_in, v),
                (q_in, q),
                (g_in, g),
            )
        )
    ]
    for fetch in fetches:
        fetch.start()
    fetches[0].wait()
    fetches[1].wait()
    w = level_weights(table, profile[...], width)
    w_out[...] = w
    fetches[2].wait()
    fetches[3].wait()
    for h in range(heads):
        lanes = slice(h * width, (h + 1) * width)
        ends_out[0, h] = contract(k[:, lanes], v[:, lanes], 0, 0)
    fetches[4].wait()
    fetches[5].wait()
    for h in range(heads):
        lanes = slice(h * width, (h + 1) * width)
        ends_out[1, h] = contract(g[:, lanes], weighted(q[:, lanes], w, h, top), 0, 0)


def second_kernel(first_far, width, heads, far, w, q, g, low_out, middle_out):
    for h in range(heads):
        lanes = slice(h * width, (h + 1) * width)
        stack = [weighted(q[:, lanes], w, h, first_far + j) for j in range(far - 1)]
        states = contract(g[:, lanes], jnp.concatenate(stack, axis=1), 0, 0)
        low_out[h] = states[:, :width]
        for j in range(1, far - 1):
            middle_out[j - 1, h] = states[:, j * width : (j + 1) * width]


def block_mask(w, levels, causal):
    parts = []
    for i in range(BLOCK // SMALL):
        rows = w[i * SMALL : (i + 1) * SMALL]
        tri = jnp.broadcast_to(rows[:, 0:1], (SMALL, SMALL))
        for l in range(1, SMALL.bit_length()):
            tri = jnp.where(levels >= l, rows[:, l : l + 1], tri)
        line = []
        for j in range(BLOCK // SMALL):
            if j > i:
                line.append(jnp.zeros((SMALL, SMALL), F32))
            elif j == i:
                line.append(jnp.where(causal, tri, 0.0))
            else:
                l = SMALL.bit_length() - 1 + (i ^ j).bit_length()
                line.append(jnp.broadcast_to(rows[:, l : l + 1], (SMALL, SMALL)))
        parts.append(jnp.concatenate(line, axis=1))
    return jnp.concatenate(parts, axis=0)


def merge_kernel(count, place, own_part, from_other, *sums):
    own = place[0]
    for l in range(count):
        taken = ((own & 1) == 1) & ((own >> l + 1 & 1) == 1)
        sums[l][...] = jnp.where(taken, own_part[l] + from_other[l], 0.0)


def tile_kernel(i, width, heads, depth, first_far, place, w, q, k, v, g, ends, out, dq, dk, dv):
    tokens = q.shape[0]
    on_first = (place[0] & 1) == 0
    places_t = lax.broadcasted_iota(jnp.int32, (SMALL, SMALL), 0)
    places_s = lax.broadcasted_iota(jnp.int32, (SMALL, SMALL), 1)
    differ = places_t ^ places_s
    levels = jnp.zeros((SMALL, SMALL), jnp.int32)
    for p in range(SMALL.bit_length() - 1):
        levels = levels + jnp.where(differ >= 1 << p, 1, 0)
    causal = places_s <= places_t
    rows = slice(i * BLOCK, (i + 1) * BLOCK)
    for h in range(heads):
        lanes = slice(h * width, (h + 1) * width)
        first = h * STRIDE
        qb, kb, vb, gb = q[rows, lanes], k[rows, lanes], v[rows, lanes], g[rows, lanes]
        mask = block_mask(w[rows, first : first + depth], levels, causal)
        probs = (contract(qb, kb, 1, 1) * mask).astype(BF16)
        grads = (contract(gb, vb, 1, 1) * mask).astype(BF16)
        state = jnp.where(on_first, 0.0, ends[0, h]).astype(BF16)
        scale = w[rows, first + first_far : first + first_far + 1]
        o = contract(probs, vb, 1, 0) + scale * contract(qb, state, 1, 0)
        d = contract(grads, kb, 1, 0) + scale * contract(gb, state, 1, 1)
        s = contract(grads, qb, 0, 0)
        e = contract(probs, gb, 0, 0)
        size = BLOCK
        while size < tokens:
            group = i * BLOCK // size
            sibling = slice((group ^ 1) * size, ((group ^ 1) + 1) * size)
            at = first + size.bit_length()
            if group & 1:
                scale = w[rows, at : at + 1]
                state = contract(k[sibling, lanes], v[sibling, lanes], 0, 0).astype(BF16)
                o = o + scale * contract(qb, state, 1, 0)
                d = d + scale * contract(gb, state, 1, 1)
            else:
                scaled = (q[sibling, lanes].astype(F32) * w[sibling, at : at + 1]).astype(BF16)
                pulled = contract(g[sibling, lanes], scaled, 0, 0).astype(BF16)
                s = s + contract(vb, pulled, 1, 0)
                e = e + contract(kb, pulled, 1, 1)
            size *= 2
        out[:, lanes] = o
        dq[:, lanes] = d
        dk[:, lanes] = s
        dv[:, lanes] = e


def far_kernel(
    width, heads, count, first_far, place, w, q, g, stacked, handed, *refs
):
    own = place[0]
    on_first = (own & 1) == 0
    local, (out, dq, near, arrived) = refs[:-4], refs[-4:]
    fetches = [pltpu.make_async_copy(part, near.at[n], arrived.at[n]) for n, part in enumerate(local)]
    for fetch in fetches:
        fetch.start()
    states = []
    for h in range(heads):
        of_head = []
        for j in range(1, count + 1):
            state = jnp.where(on_first, stacked[j - 1, h], handed[j - 1, h])
            of_head.append(jnp.where((own >> j & 1) == 1, state, 0.0).astype(BF16))
        states.append((jnp.concatenate(of_head, axis=0), jnp.concatenate(of_head, axis=1)))
    for i in range(q.shape[0] // BLOCK):
        rows = slice(i * BLOCK, (i + 1) * BLOCK)
        fetches[2 * i].wait()
        fetches[2 * i + 1].wait()
        for h in range(heads):
            lanes = slice(h * width, (h + 1) * width)
            scaled_q = [weighted(q[rows, lanes], w[rows, :], h, first_far + j) for j in range(1, count + 1)]
            scaled_g = [weighted(g[rows, lanes], w[rows, :], h, first_far + j) for j in range(1, count + 1)]
            tall, broad = states[h]
            o = contract(jnp.concatenate(scaled_q, axis=1), tall, 1, 0)
            d = contract(jnp.concatenate(scaled_g, axis=1), broad, 1, 1)
            out[rows, lanes] = near[2 * i, :, lanes] + o
            dq[rows, lanes] = near[2 * i + 1, :, lanes] + d


def more_kernel(width, heads, first, first_far, place, w, q, g, fifth, fifth_in, alone, alone_in, f_out, f_dq, out, dq):
    own = place[0]
    on_first = (own & 1) == 0
    for h in range(heads):
        lanes = slice(h * width, (h + 1) * width)
        pair, scaled_q, scaled_g = [], [], []
        for j, here, there in ((first, fifth, fifth_in), (first + 1, alone, alone_in)):
            state = jnp.where(on_first, here[h], there[h])
            pair.append(jnp.where((own >> j & 1) == 1, state, 0.0).astype(BF16))
            scaled_q.append(weighted(q[:, lanes], w, h, first_far + j))
            scaled_g.append(weighted(g[:, lanes], w, h, first_far + j))
        o = contract(jnp.concatenate(scaled_q, axis=1), jnp.concatenate(pair, axis=0), 1, 0)
        d = contract(jnp.concatenate(scaled_g, axis=1), jnp.concatenate(pair, axis=1), 1, 1)
        out[:, lanes] = f_out[:, lanes] + o
        dq[:, lanes] = f_dq[:, lanes] + d


def last_kernel(
    width, heads, far, first_far, place, w, q, k, v, g, top, final, carried, far_out, far_dq, *refs
):
    own = place[0]
    local, (out, dq, dk, dv, near, arrived, state, pulled) = refs[:-8], refs[-8:]
    step = pl.program_id(0)
    fetches = [pltpu.make_async_copy(part, near.at[n], arrived.at[n]) for n, part in enumerate(local)]

    @pl.when(step == 0)
    def _():
        for fetch in fetches:
            fetch.start()
        on_first = (own & 1) == 0
        for h in range(heads):
            highest = jnp.where(on_first, top[h], final[h])
            state[h] = jnp.where((own >> far - 1 & 1) == 1, highest, 0.0).astype(BF16)
            pulled[h] = jnp.where(on_first, final[h], carried[h]).astype(BF16)

    for n in range(q.shape[0] // SMALL):

        @pl.when(step == n)
        def _(n=n):
            i, start = n * SMALL // BLOCK, n * SMALL % BLOCK
            rows, part = slice(n * SMALL, (n + 1) * SMALL), slice(start, start + SMALL)
            if start == 0:
                fetches[2 * i].wait()
                fetches[2 * i + 1].wait()
            for h in range(heads):
                lanes = slice(h * width, (h + 1) * width)
                at = h * STRIDE + first_far + far - 1
                scale = w[rows, at : at + 1]
                out[:, lanes] = far_out[rows, lanes] + scale * contract(q[rows, lanes], state[h], 1, 0)
                dq[:, lanes] = far_dq[rows, lanes] + scale * contract(g[rows, lanes], state[h], 1, 1)
                dk[:, lanes] = near[2 * i, part, lanes] + contract(v[rows, lanes], pulled[h], 1, 0)
                dv[:, lanes] = near[2 * i + 1, part, lanes] + contract(k[rows, lanes], pulled[h], 1, 1)


def links(row_bits, col_bits):
    steps = []
    place = 1
    while place < row_bits:
        steps.append(1 << place)
        if place + 1 < row_bits:
            steps.append(3 << place)
        place += 2
    for bit in range(col_bits):
        if bit == col_bits - 1 and bit > 0:
            steps.append(3 << row_bits + bit - 1)
        else:
            steps.append(1 << row_bits + bit)
    return steps


def tie(*trees):
    return lax.optimization_barrier(trees)


def shards(row_size, col_size, queries, keys, values, out_grad, weight_table, profile):
    tokens, columns = queries.shape
    _, heads, depth = weight_table.shape
    width = columns // heads
    row_bits = row_size.bit_length() - 1
    col_bits = col_size.bit_length() - 1
    far = row_bits + col_bits
    first_far = tokens.bit_length()
    devices = row_size * col_size
    own = lax.axis_index("col") * row_size + lax.axis_index("row")
    core = own & 1
    on_first = core == 0
    profile_row = profile.reshape(1, tokens)
    table = jnp.transpose(weight_table, (2, 1, 0))

    def full(shape, kind=F32):
        return jax.ShapeDtypeStruct(shape, kind)

    square = (heads, width, width)
    unit = tokens * width * width * heads * 2
    array = tokens * columns * 2
    exchange = [(i, i ^ 1) for i in range(devices)]

    weights, ends = call(
        functools.partial(first_kernel, first_far + far - 1, width, heads),
        (full((tokens, heads * STRIDE)), full((2,) + square)),
        3 * unit,
        4 * array,
        in_specs=[HBM] * 6,
        out_specs=[VMEM] * 2,
        scratch_shapes=[
            pltpu.VMEM(profile_row.shape, jnp.int32),
            pltpu.VMEM(table.shape, F32),
        ]
        + [pltpu.VMEM((tokens, columns), BF16)] * 4
        + [pltpu.SemaphoreType.DMA((6,))],
    )(*outside(profile_row, table, queries, keys, values, out_grad))
    other = lax.ppermute(ends, AXES, exchange)

    def second(w, q, g):
        return call(
            functools.partial(second_kernel, first_far, width, heads, far),
            (full(square), full((far - 2,) + square)),
            far * unit,
            4 * array,
            in_specs=[VMEM] * 3,
        )(w, q, g)

    smem = pl.BlockSpec(memory_space=pltpu.SMEM)
    place = own.reshape(1).astype(jnp.int32)
    blocks = tokens // BLOCK

    def tile(i, *operands):
        return call(
            functools.partial(tile_kernel, i, width, heads, depth, first_far),
            [full((BLOCK, columns))] * 4,
            20 * BLOCK * BLOCK * columns,
            6 * array,
            in_specs=[smem] + [VMEM] * 5 + [pl.BlockSpec()],
        )(place, *operands)

    low_grads, middle = second(weights, queries, out_grad)
    other_middle = lax.ppermute(middle, AXES, exchange)

    def merge(own_part, from_other):
        return call(
            functools.partial(merge_kernel, far - 2),
            [full(square)] * (far - 2),
            far * width * width,
            array,
            in_specs=[smem] + [pl.BlockSpec()] * 2,
            out_specs=[VMEM] * (far - 2),
        )(place, own_part, from_other)

    def add_far(stacked, handed):
        parts = outside(*[part for i in range(blocks) for part in local[4 * i : 4 * i + 2]])
        return call(
            functools.partial(far_kernel, width, heads, far - 4, first_far),
            [full((tokens, columns))] * 2,
            2 * (far - 4) * unit,
            8 * array,
            in_specs=[smem] + [VMEM] * 3 + [pl.BlockSpec()] * 2 + [HBM] * len(parts),
            out_specs=[VMEM] * 2,
            scratch_shapes=[
                pltpu.VMEM((len(parts), BLOCK, columns), F32),
                pltpu.SemaphoreType.DMA((len(parts),)),
            ],
        )(place, weights, queries, out_grad, stacked, handed, *parts)

    steps = links(row_bits, col_bits)
    rounds = len(steps)
    carried = jnp.where(on_first, ends[0] + other[0], 0.0)
    received = []
    local = []
    for r in range(1, rounds + 1):
        if r == 1:
            is_upper = (core == 1) & ((own >> far - 1 & 1) == 1)
            send = carried + jnp.where(is_upper, ends[1] + other[1], 0.0)
            carried, send = tie(carried, send)
        else:
            send = carried + sums[far - r - 1]
        pairs = [
            (i, i ^ (steps[rounds - r] if i & 1 else steps[r - 1])) for i in range(devices)
        ]
        if r > 1:
            (send,) = tie(send)
        got = lax.ppermute(send, AXES, pairs)
        after = (got,)
        if r == 1:
            sums = merge(middle, other_middle)
            after += (sums,)
        if r <= blocks:
            part = tile(r - 1, *tie((weights, queries, keys, values, out_grad, other), send)[0])
            local += list(part)
            after += (part,)
        elif r == rounds - 2:
            stacked = jnp.stack(received)
            handed = lax.ppermute(stacked, AXES, exchange)
            after += (stacked, handed)
        elif r == rounds - 1:
            far_sums = add_far(stacked, handed)
            after += (far_sums,)
        else:
            fifth, alone = received[-2:]
            fifth_in = lax.ppermute(fifth, AXES, exchange)
            alone_in = lax.ppermute(alone, AXES, exchange)
            far_out, far_dq = call(
                functools.partial(more_kernel, width, heads, far - 3, first_far),
                [full((tokens, columns))] * 2,
                4 * unit,
                8 * array,
                in_specs=[smem] + [VMEM] * 9,
                out_specs=[VMEM] * 2,
            )(
                place, weights, queries, out_grad, fifth, fifth_in, alone, alone_in,
                *far_sums,
            )
            after += (far_out, far_dq)
        after = tie(*after)
        got = after[0]
        if r == 1:
            sums = after[1]
        if r == rounds - 1:
            far_sums = after[1]
        if r == rounds:
            far_out, far_dq = after[1:]
        received.append(got)
        carried = carried + got

    top = received[-1]
    final = lax.ppermute(jnp.where(on_first, top, carried + low_grads), AXES, exchange)

    wide = pl.BlockSpec((SMALL, columns), lambda i: (i, 0))
    seconds = outside(*[part for i in range(blocks) for part in local[4 * i + 2 : 4 * i + 4]])
    return call(
        functools.partial(last_kernel, width, heads, far, first_far),
        [full((tokens, columns))] * 4,
        6 * unit,
        16 * array,
        grid=(tokens // SMALL,),
        in_specs=[smem] + [VMEM] * 5 + [pl.BlockSpec()] * 3 + [VMEM] * 2 + [HBM] * len(seconds),
        out_specs=[wide] * 4,
        scratch_shapes=[
            pltpu.VMEM((len(seconds), BLOCK, columns), F32),
            pltpu.SemaphoreType.DMA((len(seconds),)),
            pltpu.VMEM(square, BF16),
            pltpu.VMEM(square, BF16),
        ],
    )(
        place, weights, queries, keys, values, out_grad, top, final, carried,
        far_out, far_dq, *seconds,
    )


def solution(mesh):
    spread = P(AXES, None)

    def body(*args):
        return shards(mesh.shape["row"], mesh.shape["col"], *args)

    return jax.shard_map(
        body,
        mesh=mesh,
        in_specs=(spread,) * 4 + (P(), P(AXES)),
        out_specs=(spread,) * 4,
        check_vma=False,
    )
```
